256 devices in a mesh: region: 32 (over y_hi, z, core), tracer: 8 (over y_lo, x).
Axes of the slice: x: 4, y: 4 (y_hi: 2, y_lo: 2; y = y_hi * 2 + y_lo), z: 8, core: 2. Of those that a mesh axis runs over, the one named last changes fastest.
Arguments:
- tracers: float32 [256, 64, 6144], P('tracer', 'region'), may hold values from 0.2 to 1.5
- fluxes: float32 [2, 64, 6144], P(None, 'region', 'tracer'), may hold values from -0.4 to 0.4
- rate_coeff: float32 [1024], replicated, may hold values from 0.005 to 0.05
- first_reactant: int32 [1024], replicated, may hold values from 0 to 255
- second_reactant: int32 [1024], replicated, may hold values from 0 to 255
- product_species: int32 [1024], replicated, may hold values from 0 to 255
Outputs:
- tracers_out: float32 [256, 64, 6144], P('tracer', 'region')
The draws below stay inside these ranges and needn't reach their ends.
All inputs are finite; a program needn't handle non-finite values.
Results may differ from the reference program's by a relative error of at most 0.0001.
Values sent between devices are 32-bit elements; how exact they have to be, the bound alone decides.
No kernel may reach another device: no remote copies, remote signals or barrier semaphores. Data moves between devices by JAX's collectives and lax.ppermute only.
A program may use at most 64 MiB of HBM per device.

```python
import math
import jax
import jax.numpy as jnp
from jax import lax

TRACERS = 256
REACTIONS = 1024
NY = 48
LEV = 128
CX = 2
ADV_STEPS = 2
SUBSTEPS = 4
NX = 64


def set_ends(values, rng, low, top_value):
    dims = values.shape
    place = [jax.random.randint(jax.random.fold_in(rng, axis), (), 0, dims[axis]) for axis in range(len(dims))]
    values = values.at[tuple(place)].set(low)
    longest = dims.index(max(dims))
    place[longest] = (place[longest] + 1) % dims[longest]
    return values.at[tuple(place)].set(top_value)


def steps_of(key, dims, split, least, largest):
    def one(dim, shards_of):
        steps = jax.random.uniform(jax.random.fold_in(jax.random.fold_in(key, 6), dim), (shards_of,), jnp.float32, least / len(split), largest / len(split))
        return jnp.repeat(jnp.exp(steps), dims[dim] // shards_of).reshape((-1,) + (1,) * (len(dims) - dim - 1))

    factor_of = one(*split[0])
    for cut in split[1:]:
        factor_of = factor_of * one(*cut)
    return factor_of


def setup_inputs(seed: int = 0) -> dict:
    key_list = jax.random.split(jax.random.key(seed), 7)
    tracers = jnp.clip(0.2 + 1.3 * jax.random.uniform(key_list[0], (TRACERS, NX, LEV * NY), jnp.float32) ** steps_of(key_list[0], (TRACERS, NX, LEV * NY), ((0, 8), (1, 32)), -0.2, 0.2), 0.2, 1.5)
    fluxes = jnp.clip(jax.random.uniform(key_list[1], (2, NX, LEV * NY), jnp.float32, -0.4, 0.4) * steps_of(key_list[1], (2, NX, LEV * NY), ((1, 32), (2, 8)), -0.4, 0.0), -0.4, 0.4)
    rate_coeff = jnp.clip(jnp.exp(jax.random.uniform(key_list[2], (REACTIONS,), jnp.float32, math.log(0.005), math.log(0.05))), 0.005, 0.05)
    first_reactant = set_ends(jax.random.randint(key_list[3], (REACTIONS,), 0, TRACERS), jax.random.fold_in(key_list[3], 1), 0, TRACERS - 1).astype(jnp.int32)
    second_reactant = set_ends(jax.random.randint(key_list[4], (REACTIONS,), 0, TRACERS), jax.random.fold_in(key_list[4], 1), 0, TRACERS - 1).astype(jnp.int32)
    product_species = set_ends(jax.random.randint(key_list[5], (REACTIONS,), 0, TRACERS), jax.random.fold_in(key_list[5], 1), 0, TRACERS - 1).astype(jnp.int32)
    return {"tracers": tracers, "fluxes": fluxes, "rate_coeff": rate_coeff, "first_reactant": first_reactant, "second_reactant": second_reactant, "product_species": product_species}


def advect(padded, courant, margin, wind_margin, row_len):
    length = padded.shape[1]
    offset = wind_margin - margin
    east_flow = courant[0, offset + 1: offset + length]
    flux_x = jnp.maximum(east_flow, 0.0) * padded[:, :-1] + jnp.minimum(east_flow, 0.0) * padded[:, 1:]
    central = padded[:, 1:-1]
    north_flow = courant[1, offset + 1: offset + length - 1]
    south_cell = jnp.roll(central, 1, axis=2)
    y_index = jnp.arange(central.shape[2], dtype=jnp.int32) % row_len
    flux_y = jnp.where(y_index == 0, 0.0, jnp.maximum(north_flow, 0.0) * south_cell + jnp.minimum(north_flow, 0.0) * central)
    return central + flux_x[:, :-1] - flux_x[:, 1:] + flux_y - jnp.roll(flux_y, -1, axis=2)


def tables(first_reactant, second_reactant, product_species, count):
    species = jnp.arange(count, dtype=jnp.int32)
    pick_first = (first_reactant[:, None] == species[None, :]).astype(jnp.float32)
    pick_second = (second_reactant[:, None] == species[None, :]).astype(jnp.float32)
    made = (product_species[:, None] == species[None, :]).astype(jnp.float32)
    change_table = jnp.transpose(made - pick_first - pick_second)
    return pick_first, pick_second, change_table


def chemistry_steps(amounts, rate_coeff, pick_first, pick_second, change_table):
    for repeat in range(SUBSTEPS):
        first = jnp.dot(pick_first, amounts, precision=lax.Precision.HIGHEST)
        second = jnp.dot(pick_second, amounts, precision=lax.Precision.HIGHEST)
        velocity = rate_coeff[:, None] * first * second
        amounts = amounts + jnp.dot(change_table, velocity, precision=lax.Precision.HIGHEST)
    return amounts


def reference(tracers, fluxes, rate_coeff, first_reactant, second_reactant, product_species):
    courant = jnp.concatenate([fluxes[:, -ADV_STEPS:], fluxes, fluxes[:, :ADV_STEPS]], axis=1)
    tracer_now = tracers
    for repeat in range(ADV_STEPS):
        padded = jnp.concatenate([tracer_now[:, -1:], tracer_now, tracer_now[:, :1]], axis=1)
        tracer_now = advect(padded, courant, 1, ADV_STEPS, NY)
    pick_first, pick_second, change_table = tables(first_reactant, second_reactant, product_species, TRACERS)
    block_size = CX * LEV * NY
    by_block = jnp.transpose(tracer_now.reshape(TRACERS, -1, block_size), (1, 0, 2))

    def chemistry(portion):
        return chemistry_steps(portion, rate_coeff, pick_first, pick_second, change_table)

    reacted = lax.map(chemistry, by_block)
    return jnp.transpose(reacted, (1, 0, 2)).reshape(tracer_now.shape)
```

```python
import jax
import jax.numpy as jnp
from jax import lax
from jax.experimental import pallas as pl
from jax.experimental.pallas import tpu as pltpu
from jax.sharding import Mesh, PartitionSpec as P

TRACERS = 256
NY = 48
SUBSTEPS = 4
CHUNKS = 2
F32 = jnp.float32
BF16 = jnp.bfloat16
PLANE = ("yhi", "tracer")
RING = ("z", "core")


def gather_kernel(x_ref, o_ref):
    cols = x_ref.shape[1]
    half = x_ref.shape[2] // 2
    for h in range(2):
        for c in range(cols):
            o_ref[h, 0, :, c * half : (c + 1) * half] = x_ref[:, c, h * half : (h + 1) * half]


def to_blocks(tracers, chunk, groups):
    own, cols, length = tracers.shape
    width = length // groups // CHUNKS
    return pl.pallas_call(
        gather_kernel,
        grid=(groups,),
        in_specs=[pl.BlockSpec((own, cols, width), lambda t: (0, 0, t * CHUNKS + chunk))],
        out_specs=pl.BlockSpec((2, 1, own, width), lambda t: (0, t, 0, 0)),
        out_shape=jax.ShapeDtypeStruct((2, groups, own, width), F32),
        name="to_blocks",
    )(tracers)


def scatter_body(y_ref, o_ref):
    cols = o_ref.shape[1]
    half = o_ref.shape[2] // 2
    for h in range(2):
        for c in range(cols):
            o_ref[:, c, h * half : (h + 1) * half] = y_ref[h, 0, :, c * half : (c + 1) * half]


def scatter_more(y_ref, so_far, o_ref):
    scatter_body(y_ref, o_ref)


def from_blocks(blocks, so_far, chunk, shape):
    own, cols, length = shape
    groups = blocks.shape[1]
    width = blocks.shape[3]
    in_specs = [pl.BlockSpec((2, 1, own, width), lambda t: (0, t, 0, 0))]
    args = [blocks]
    if so_far is not None:
        in_specs.append(pl.BlockSpec(memory_space=pl.ANY))
        args.append(so_far)
    return pl.pallas_call(
        scatter_body if so_far is None else scatter_more,
        grid=(groups,),
        in_specs=in_specs,
        out_specs=pl.BlockSpec((own, cols, width), lambda t: (0, 0, t * CHUNKS + chunk)),
        out_shape=jax.ShapeDtypeStruct(shape, F32),
        input_output_aliases={} if so_far is None else {1: 0},
        name="from_blocks",
    )(*args)


def split(values):
    high = values.astype(BF16)
    low = (values - high.astype(F32)).astype(BF16)
    return high, low


def react_kernel(swap, own, left, right, wide, narrow, pick1, pick2, change, rates, out, cells):
    width = own.shape[2]
    col = width // 2
    rows = 32

    for h in range(2):
        from_left = jnp.where(swap[0] == 1, 1 - h, h)
        from_right = jnp.where(swap[1] == 1, 1 - h, h)

        def move(i, carry):
            at = pl.ds(pl.multiple_of(i * rows, rows), rows)
            q = jnp.concatenate([left[from_left, at, :], own[h, at, :], right[from_right, at, :]], axis=1)
            n = 4 * col
            q = (
                wide[h, 0:1, :] * q[:, col : col + n]
                + wide[h, 1:2, :] * q[:, 0:n]
                + wide[h, 2:3, :] * q[:, 2 * col : 2 * col + n]
                + wide[h, 3:4, :] * q[:, col - 1 : col - 1 + n]
                + wide[h, 4:5, :] * q[:, col + 1 : col + 1 + n]
            )
            n = 2 * col
            q = (
                narrow[h, 0:1, :] * q[:, col : col + n]
                + narrow[h, 1:2, :] * q[:, 0:n]
                + narrow[h, 2:3, :] * q[:, 2 * col : 2 * col + n]
                + narrow[h, 3:4, :] * q[:, col - 1 : col - 1 + n]
                + narrow[h, 4:5, :] * q[:, col + 1 : col + 1 + n]
            )
            cells[at, h * width : (h + 1) * width] = q
            return carry

        lax.fori_loop(0, own.shape[1] // rows, move, 0)

    amounts = cells[...]
    for step in range(SUBSTEPS):
        parts = jnp.concatenate(split(amounts), axis=0)
        first = jnp.dot(pick1[...], parts, preferred_element_type=F32)
        second = jnp.dot(pick2[...], parts, preferred_element_type=F32)
        rate = jnp.concatenate([rates[...]] * (amounts.shape[1] // rates.shape[1]), axis=1)
        velocity = jnp.concatenate(split(rate * first * second), axis=0)
        amounts = amounts + jnp.dot(change[...], velocity, preferred_element_type=F32)
    for h in range(2):
        out[h] = amounts[:, h * width : (h + 1) * width]


def react(swap, own, left, right, wide, narrow, pick1, pick2, change, rates):
    vmem = pl.BlockSpec(memory_space=pltpu.VMEM)
    return pl.pallas_call(
        react_kernel,
        in_specs=[pl.BlockSpec(memory_space=pltpu.SMEM)] + [vmem] * 9,
        out_specs=vmem,
        out_shape=jax.ShapeDtypeStruct(own.shape, F32),
        scratch_shapes=[pltpu.VMEM((own.shape[1], 2 * own.shape[2]), F32)],
        compiler_params=pltpu.CompilerParams(vmem_limit_bytes=48 << 20),
        name="react",
    )(swap, own, left, right, wide, narrow, pick1, pick2, change, rates)


def coefficients(winds, start, length):
    east, north = winds[..., 0, :], winds[..., 1, :]
    col = winds.shape[-1] // 6

    def window(array, shift):
        return lax.slice_in_dim(array, start + shift, start + shift + length, axis=-1)

    row = jnp.arange(length, dtype=jnp.int32) % NY
    u, u_next = window(east, 0), window(east, col)
    v = jnp.where(row == 0, 0.0, window(north, 0))
    v_next = jnp.where(row == NY - 1, 0.0, window(north, 1))
    here = (
        1.0
        + jnp.minimum(u, 0.0)
        - jnp.maximum(u_next, 0.0)
        + jnp.minimum(v, 0.0)
        - jnp.maximum(v_next, 0.0)
    )
    return jnp.stack(
        [
            here,
            jnp.maximum(u, 0.0),
            -jnp.minimum(u_next, 0.0),
            jnp.maximum(v, 0.0),
            -jnp.minimum(v_next, 0.0),
        ],
        axis=-2,
    )


def neighbours(array):
    count = lax.axis_size(RING)
    left = lax.ppermute(array, RING, [(i, (i + 1) % count) for i in range(count)])
    right = lax.ppermute(array, RING, [((i + 1) % count, i) for i in range(count)])
    return left, right


def body(tracers, fluxes, rate_coeff, first_reactant, second_reactant, product_species):
    groups = lax.axis_size("tracer")
    count = lax.axis_size(RING)
    place = lax.axis_index(RING)
    swap = jnp.stack([place == 0, place == count - 1]).astype(jnp.int32)

    gathered = []
    for chunk in range(CHUNKS):
        blocks = to_blocks(tracers, chunk, groups).reshape(2 * groups, tracers.shape[0], -1)
        gathered.append(lax.all_to_all(blocks, PLANE, split_axis=0, concat_axis=0, tiled=True))

    cols = fluxes.shape[1]
    winds = fluxes.reshape(2, cols, CHUNKS, 2, -1)
    winds = jnp.transpose(winds, (3, 2, 0, 1, 4))
    winds = lax.all_to_all(winds, "yhi", split_axis=0, concat_axis=0, tiled=True)
    winds = winds.reshape(2, CHUNKS, 2, -1)
    left, right = neighbours(winds)
    left = jnp.where(place == 0, left[::-1], left)
    right = jnp.where(place == count - 1, right[::-1], right)
    winds = jnp.concatenate([left, winds, right], axis=-1)
    col = winds.shape[-1] // 6
    wide = coefficients(winds, col, 4 * col)
    narrow = coefficients(winds, 2 * col, 2 * col)

    species = jnp.arange(2 * TRACERS, dtype=jnp.int32) % TRACERS
    pick1 = (first_reactant[:, None] == species[None, :]).astype(BF16)
    pick2 = (second_reactant[:, None] == species[None, :]).astype(BF16)
    kinds = jnp.arange(TRACERS, dtype=jnp.int32)[:, None]
    change = (
        (product_species[None, :] == kinds).astype(F32)
        - (first_reactant[None, :] == kinds).astype(F32)
        - (second_reactant[None, :] == kinds).astype(F32)
    ).astype(BF16)
    change = jnp.concatenate([change, change], axis=1)
    rates = jnp.broadcast_to(rate_coeff[:, None], (rate_coeff.shape[0], 128))

    out = None
    for chunk in range(CHUNKS):
        own = gathered[chunk]
        left, right = neighbours(own)
        shape = (2, TRACERS, own.shape[-1])
        reacted = react(
            swap,
            own.reshape(shape),
            left.reshape(shape),
            right.reshape(shape),
            wide[:, chunk],
            narrow[:, chunk],
            pick1,
            pick2,
            change,
            rates,
        )
        back = lax.all_to_all(reacted.reshape(own.shape), PLANE, split_axis=0, concat_axis=0, tiled=True)
        out = from_blocks(back.reshape(2, groups, tracers.shape[0], -1), out, chunk, tracers.shape)
    return out


def solution(mesh):
    regions, groups = mesh.devices.shape
    torus = Mesh(mesh.devices.reshape(2, regions // 4, 2, groups), ("yhi", "z", "core", "tracer"))
    region = ("yhi", "z", "core")
    in_specs = (P("tracer", region, None), P(None, region, "tracer"), P(), P(), P(), P())
    out_specs = P("tracer", region, None)
    return jax.shard_map(body, mesh=torus, in_specs=in_specs, out_specs=out_specs, check_vma=False)
```

```python
import jax
import jax.numpy as jnp
from jax import lax
from jax.experimental import pallas as pl
from jax.experimental.pallas import tpu as pltpu
from jax.sharding import PartitionSpec as P

TRACERS = 256
NY = 48
SUBSTEPS = 4
LANES = 128
CHUNKS = 2
F32 = jnp.float32
BF16 = jnp.bfloat16
VMEM = pl.BlockSpec(memory_space=pltpu.VMEM)


def as_tiles(tracers):
    own, cols, length = tracers.shape
    tiles = tracers.reshape(own, cols, length // LANES, LANES)
    return jnp.transpose(tiles, (0, 2, 1, 3)).reshape(-1, LANES).reshape(own, -1, LANES)


def cut_kernel(x_ref, *o_refs):
    part = o_refs[0].shape[1]
    for k, o_ref in enumerate(o_refs):
        o_ref[...] = x_ref[:, k * part : (k + 1) * part, :]


def cut(tiles):
    own, length, _ = tiles.shape
    part = length // CHUNKS
    parts = pl.pallas_call(
        cut_kernel,
        grid=(own // 8,),
        in_specs=[pl.BlockSpec((8, length, LANES), lambda i: (i, 0, 0))],
        out_specs=[pl.BlockSpec((8, part, LANES), lambda i: (i, 0, 0))] * CHUNKS,
        out_shape=[jax.ShapeDtypeStruct((own, part, LANES), F32)] * CHUNKS,
        name="cut",
    )(tiles)
    return [array.reshape(own * part, LANES) for array in parts]


def from_tiles(tiles, shape):
    own, cols, length = shape
    tiles = tiles.reshape(own, length // LANES, cols, LANES)
    return jnp.transpose(tiles, (0, 2, 1, 3)).reshape(shape)


def transport_kernel(winds, left, own, right, out):
    groups, count, twice = out.shape
    width = twice // 2
    pieces = width // LANES
    stride = own.shape[0] // count
    pairs = winds.shape[3] // width
    rows = 16
    y = lax.rem(lax.broadcasted_iota(jnp.int32, (4, width), 1), NY)

    def south(array):
        return pltpu.roll(array, 1, 1)

    def north(array):
        return pltpu.roll(array, width - 1, 1)

    def at_source(u, carry):
        for half in range(pairs):
            t = u * pairs + half
            lanes = slice(half * width, (half + 1) * width)
            east = winds[u, 0, 1:5, lanes]
            east_next = winds[u, 0, 2:6, lanes]
            upward = winds[u, 1, 1:5, lanes]
            upward_next = jnp.where(y == NY - 1, 0.0, north(upward))
            upward = jnp.where(y == 0, 0.0, upward)
            here = (
                1.0
                + jnp.minimum(east, 0.0)
                - jnp.maximum(east_next, 0.0)
                + jnp.minimum(upward, 0.0)
                - jnp.maximum(upward_next, 0.0)
            )
            west_of = jnp.maximum(east, 0.0)
            east_of = -jnp.minimum(east_next, 0.0)
            south_of = jnp.maximum(upward, 0.0)
            north_of = -jnp.minimum(upward_next, 0.0)

            def step(q, at, west, east):
                row = slice(at, at + 1)
                return (
                    here[row] * q
                    + west_of[row] * west
                    + east_of[row] * east
                    + south_of[row] * south(q)
                    + north_of[row] * north(q)
                )

            for first in range(0, count, rows):

                def column(ref, c):
                    start = first * stride + 2 * pieces * t + c
                    return jnp.concatenate(
                        [ref[pl.ds(start + 2 * m, rows, stride=stride), :] for m in range(pieces)], axis=1
                    )

                q = [column(ref, c) for ref in (left, own, right) for c in range(2)]
                q = [step(q[i + 1], i, q[i], q[i + 2]) for i in range(4)]
                for c in range(2):
                    out[t, first : first + rows, c * width : (c + 1) * width] = step(
                        q[c + 1], c + 1, q[c], q[c + 2]
                    )
        return carry

    lax.fori_loop(0, winds.shape[0], at_source, 0)


def transport(winds, left, own, right, shape):
    return pl.pallas_call(
        transport_kernel,
        in_specs=[VMEM] * 4,
        out_specs=VMEM,
        out_shape=jax.ShapeDtypeStruct(shape, F32),
        compiler_params=pltpu.CompilerParams(vmem_limit_bytes=32 << 20),
        name="transport",
    )(winds, left, own, right)


def join_kernel(*refs):
    *y_refs, x_ref = refs
    groups, rows, twice = y_refs[0].shape
    width = twice // 2
    pieces = width // LANES
    stride = x_ref.shape[0] // rows
    for chunk, y_ref in enumerate(y_refs):
        for t in range(groups):
            for c in range(2):
                for m in range(pieces):
                    at = chunk * (stride // CHUNKS) + 2 * (t * pieces + m) + c
                    lane = c * width + m * LANES
                    x_ref[pl.ds(at, rows, stride=stride), :] = y_ref[t, :, lane : lane + LANES]


def join(blocks, shape):
    own, cols, length = shape
    groups, _, twice = blocks[0].shape
    rows = own * cols * length // LANES
    steps = own // 8
    tiles = pl.pallas_call(
        join_kernel,
        grid=(steps,),
        in_specs=[pl.BlockSpec((groups, 8, twice), lambda i: (0, i, 0))] * CHUNKS,
        out_specs=pl.BlockSpec((rows // steps, LANES), lambda i: (i, 0)),
        out_shape=jax.ShapeDtypeStruct((rows, LANES), F32),
        name="join",
    )(*blocks)
    return from_tiles(tiles, shape)


def split(values):
    high = values.astype(BF16)
    low = (values - high.astype(F32)).astype(BF16)
    return jnp.concatenate([high, low], axis=0)


def react_kernel(cells, pick1, pick2, change, rates, out):
    amounts = cells[...]
    rate = jnp.concatenate([rates[...]] * (amounts.shape[1] // LANES), axis=1)
    for step in range(SUBSTEPS):
        parts = split(amounts)
        first = jnp.dot(pick1[...], parts, preferred_element_type=F32)
        second = jnp.dot(pick2[...], parts, preferred_element_type=F32)
        velocity = split(rate * first * second)
        amounts = amounts + jnp.dot(change[...], velocity, preferred_element_type=F32)
    out[...] = amounts


def react(cells, pick1, pick2, change, rates):
    return pl.pallas_call(
        react_kernel,
        in_specs=[VMEM] * 5,
        out_specs=VMEM,
        out_shape=jax.ShapeDtypeStruct(cells.shape, F32),
        compiler_params=pltpu.CompilerParams(vmem_limit_bytes=48 << 20),
        name="react",
    )(cells, pick1, pick2, change, rates)


def neighbours(array):
    count = lax.axis_size("region")
    left = lax.ppermute(array, "region", [(i, (i + 1) % count) for i in range(count)])
    right = lax.ppermute(array, "region", [((i + 1) % count, i) for i in range(count)])
    return left, right


def tables(first_reactant, second_reactant, product_species, rate_coeff):
    species = jnp.arange(2 * TRACERS, dtype=jnp.int32) % TRACERS
    pick1 = (first_reactant[:, None] == species[None, :]).astype(BF16)
    pick2 = (second_reactant[:, None] == species[None, :]).astype(BF16)
    kinds = jnp.arange(TRACERS, dtype=jnp.int32)[:, None]
    change = (
        (product_species[None, :] == kinds).astype(F32)
        - (first_reactant[None, :] == kinds).astype(F32)
        - (second_reactant[None, :] == kinds).astype(F32)
    ).astype(BF16)
    change = jnp.concatenate([change, change], axis=1)
    rates = jnp.broadcast_to(rate_coeff[:, None], (rate_coeff.shape[0], LANES))
    return pick1, pick2, change, rates


def exchange(blocks):
    return lax.all_to_all(blocks, "tracer", split_axis=0, concat_axis=0, tiled=True)


def body(tracers, fluxes, rate_coeff, first_reactant, second_reactant, product_species):
    groups = lax.axis_size("tracer")
    count, cols, length = tracers.shape
    width = length // groups // CHUNKS

    own = cut(as_tiles(tracers))
    left, right = neighbours(fluxes)
    winds = lax.all_gather(jnp.concatenate([left, fluxes, right], axis=1), "tracer")
    sides = [neighbours(array) for array in own]
    table = tables(first_reactant, second_reactant, product_species, rate_coeff)
    winds, table = lax.optimization_barrier((winds, table))

    per = groups // CHUNKS
    returned = []
    for k in range(CHUNKS):
        left, right = sides[k]
        moved = transport(
            winds[k * per : (k + 1) * per], left, own[k], right, (groups, count, cols * width)
        )
        cells = exchange(moved).reshape(groups * count, cols * width)
        reacted = react(cells, *table)
        returned.append(exchange(reacted.reshape(groups, count, cols * width)))
    return join(returned, tracers.shape)


def solution(mesh):
    in_specs = (P("tracer", "region", None), P(None, "region", "tracer"), P(), P(), P(), P())
    out_specs = P("tracer", "region", None)
    return jax.shard_map(body, mesh=mesh, in_specs=in_specs, out_specs=out_specs, check_vma=False)
```

```python
import functools

import jax
import jax.numpy as jnp
from jax import lax
from jax.experimental import pallas as pl
from jax.experimental.pallas import tpu as pltpu
from jax.sharding import PartitionSpec as P

TRACERS = 256
NY = 48
SUBSTEPS = 4
LANES = 128
CHUNKS = 2
F32 = jnp.float32
BF16 = jnp.bfloat16
VMEM = pl.BlockSpec(memory_space=pltpu.VMEM)


def as_tiles(tracers):
    own, cols, length = tracers.shape
    tiles = tracers.reshape(own, cols, length // LANES, LANES)
    return jnp.transpose(tiles, (0, 2, 1, 3)).reshape(-1, LANES)


def from_tiles(tiles, shape):
    own, cols, length = shape
    tiles = tiles.reshape(own, length // LANES, cols, LANES)
    return jnp.transpose(tiles, (0, 2, 1, 3)).reshape(shape)


def transport_kernel(chunk, before, winds, after, left, own, right, out):
    pairs, count, twice = out.shape
    width = twice // 2
    pieces = width // LANES
    stride = own.shape[0] // count
    rows = 16
    y = lax.rem(lax.broadcasted_iota(jnp.int32, (4, width), 1), NY)
    u = pl.program_id(0)
    source = u + chunk * pl.num_programs(0)

    def south(array):
        return pltpu.roll(array, 1, 1)

    def north(array):
        return pltpu.roll(array, width - 1, 1)

    for half in range(pairs):
        t = u * pairs + half
        lanes = slice(half * width, (half + 1) * width)

        def around(kind, first):
            faces = [
                before[source, kind, 1:2, lanes],
                winds[source, kind, 0:2, lanes],
                after[source, kind, 0:2, lanes],
            ]
            return jnp.concatenate(faces, axis=0)[first : first + 4]

        east = around(0, 0)
        east_next = around(0, 1)
        upward = around(1, 0)
        upward_next = jnp.where(y == NY - 1, 0.0, north(upward))
        upward = jnp.where(y == 0, 0.0, upward)
        here = (
            1.0
            + jnp.minimum(east, 0.0)
            - jnp.maximum(east_next, 0.0)
            + jnp.minimum(upward, 0.0)
            - jnp.maximum(upward_next, 0.0)
        )
        west_of = jnp.maximum(east, 0.0)
        east_of = -jnp.minimum(east_next, 0.0)
        south_of = jnp.maximum(upward, 0.0)
        north_of = -jnp.minimum(upward_next, 0.0)

        def step(q, at, west, east):
            row = slice(at, at + 1)
            return (
                here[row] * q
                + west_of[row] * west
                + east_of[row] * east
                + south_of[row] * south(q)
                + north_of[row] * north(q)
            )

        for first in range(0, count, rows):

            def column(ref, c):
                start = first * stride + 2 * pieces * t + c
                return jnp.concatenate(
                    [ref[pl.ds(start + 2 * m, rows, stride=stride), :] for m in range(pieces)], axis=1
                )

            q = [column(ref, c) for ref in (left, own, right) for c in range(2)]
            q = [step(q[i + 1], i, q[i], q[i + 2]) for i in range(4)]
            for c in range(2):
                out[half, first : first + rows, c * width : (c + 1) * width] = step(
                    q[c + 1], c + 1, q[c], q[c + 2]
                )


def transport(chunk, winds, left, own, right, shape):
    groups, count, twice = shape
    steps = groups // CHUNKS
    return pl.pallas_call(
        functools.partial(transport_kernel, chunk),
        grid=(steps,),
        in_specs=[VMEM] * 6,
        out_specs=pl.BlockSpec((groups // steps, count, twice), lambda u: (u, 0, 0)),
        out_shape=pltpu.HBM(shape, F32),
        compiler_params=pltpu.CompilerParams(vmem_limit_bytes=16 << 20),
        name="transport",
    )(*winds, left, own, right)


def join_kernel(y_ref, *refs):
    x_ref = refs[-1]
    groups, _, twice = y_ref.shape
    rows = x_ref.shape[0]
    at = pl.ds(pl.multiple_of(pl.program_id(0) * rows, rows), rows)
    width = twice // 2
    pieces = width // LANES
    stride = x_ref.shape[1]
    flat = x_ref.reshape(rows * stride, LANES)
    for t in range(groups):
        for c in range(2):
            for m in range(pieces):
                lane = c * width + m * LANES
                flat[pl.ds(2 * (t * pieces + m) + c, rows, stride=stride), :] = y_ref[t, at, lane : lane + LANES]


def join(blocks, so_far, chunk):
    groups, own, twice = blocks.shape
    length = groups * twice // LANES
    more = [] if so_far is None else [so_far]
    return pl.pallas_call(
        join_kernel,
        grid=(own // 8,),
        in_specs=[VMEM]
        + [pl.BlockSpec(memory_space=pl.ANY)] * len(more),
        out_specs=pl.BlockSpec((8, length, LANES), lambda i: (i, chunk, 0)),
        out_shape=jax.ShapeDtypeStruct((own, CHUNKS * length, LANES), F32),
        input_output_aliases={1: 0} if more else {},
        name="join",
    )(blocks, *more)


def split(values):
    high = values.astype(BF16)
    low = (values - high.astype(F32)).astype(BF16)
    return jnp.concatenate([high, low], axis=0)


def react_kernel(cells, pick1, pick2, change, rates, out):
    amounts = cells[...]
    rate = jnp.concatenate(
        [jnp.broadcast_to(rates[i : i + 1, :], (LANES, LANES)).T for i in range(rates.shape[0])], axis=0
    )
    rate = jnp.concatenate([rate] * (amounts.shape[1] // LANES), axis=1)
    for step in range(SUBSTEPS):
        parts = split(amounts)
        first = jnp.dot(pick1[...], parts, preferred_element_type=F32)
        second = jnp.dot(pick2[...], parts, preferred_element_type=F32)
        velocity = split(rate * first * second)
        amounts = amounts + jnp.dot(change[...], velocity, preferred_element_type=F32)
    out[...] = amounts


def react(cells, pick1, pick2, change, rates):
    return pl.pallas_call(
        react_kernel,
        in_specs=[VMEM] * 5,
        out_specs=VMEM,
        out_shape=jax.ShapeDtypeStruct(cells.shape, F32),
        compiler_params=pltpu.CompilerParams(vmem_limit_bytes=24 << 20),
        name="react",
    )(cells, pick1, pick2, change, rates)


def neighbours(array):
    count = lax.axis_size("region")
    left = lax.ppermute(array, "region", [(i, (i + 1) % count) for i in range(count)])
    right = lax.ppermute(array, "region", [((i + 1) % count, i) for i in range(count)])
    return left, right


def tables(first_reactant, second_reactant, product_species, rate_coeff):
    species = jnp.arange(2 * TRACERS, dtype=jnp.int32) % TRACERS
    pick1 = (first_reactant[:, None] == species[None, :]).astype(BF16)
    pick2 = (second_reactant[:, None] == species[None, :]).astype(BF16)
    kinds = jnp.arange(TRACERS, dtype=jnp.int32)[:, None]
    change = (
        (product_species[None, :] == kinds).astype(F32)
        - (first_reactant[None, :] == kinds).astype(F32)
        - (second_reactant[None, :] == kinds).astype(F32)
    ).astype(BF16)
    change = jnp.concatenate([change, change], axis=1)
    return pick1, pick2, change, rate_coeff.reshape(-1, LANES)


def exchange(blocks):
    return lax.all_to_all(blocks, "tracer", split_axis=0, concat_axis=0, tiled=True)


def body(tracers, fluxes, rate_coeff, first_reactant, second_reactant, product_species):
    groups = lax.axis_size("tracer")
    count, cols, length = tracers.shape
    width = length // groups // CHUNKS

    part = length // CHUNKS
    own = [as_tiles(lax.slice_in_dim(tracers, k * part, (k + 1) * part, axis=2)) for k in range(CHUNKS)]
    section = exchange(jnp.broadcast_to(fluxes, (groups, *fluxes.shape)))
    before, after = neighbours(section)
    winds = (before, section, after)
    sides = [neighbours(array) for array in own]
    table = tables(first_reactant, second_reactant, product_species, rate_coeff)
    winds, table = lax.optimization_barrier((winds, table))

    out = None
    for k in range(CHUNKS):
        left, right = sides[k]
        moved = transport(k, winds, left, own[k], right, (groups, count, cols * width))
        cells = exchange(moved).reshape(groups * count, cols * width)
        reacted = react(cells, *table)
        back = exchange(reacted.reshape(groups, count, cols * width))
        out = join(back, out, k)
    return from_tiles(out, tracers.shape)


def solution(mesh):
    in_specs = (P("tracer", "region", None), P(None, "region", "tracer"), P(), P(), P(), P())
    out_specs = P("tracer", "region", None)
    return jax.shard_map(body, mesh=mesh, in_specs=in_specs, out_specs=out_specs, check_vma=False)
```

```python
import functools

import jax
import jax.numpy as jnp
from jax import lax
from jax.experimental import pallas as pl
from jax.experimental.pallas import tpu as pltpu
from jax.sharding import PartitionSpec as P

TRACERS = 256
NY = 48
SUBSTEPS = 4
LANES = 128
CHUNKS = 2
F32 = jnp.float32
BF16 = jnp.bfloat16
VMEM = pl.BlockSpec(memory_space=pltpu.VMEM)


def as_tiles(tracers):
    own, cols, length = tracers.shape
    tiles = tracers.reshape(own, cols, length // LANES, LANES)
    return jnp.transpose(tiles, (0, 2, 1, 3)).reshape(-1, LANES)


def from_tiles(tiles, shape):
    own, cols, length = shape
    tiles = tiles.reshape(own, length // LANES, cols, LANES)
    return jnp.transpose(tiles, (0, 2, 1, 3)).reshape(shape)


def transport_kernel(chunk, winds, left, own, right, out):
    ahead, count, twice = out.shape
    width = twice // 2
    pieces = width // LANES
    stride = own.shape[1]
    pairs = winds.shape[4] // width
    rows = 16
    y = lax.rem(lax.broadcasted_iota(jnp.int32, (4, width), 1), NY)
    steps = pl.num_programs(0)
    sources = ahead // pairs
    left, own, right = (ref.reshape(count * stride, LANES) for ref in (left, own, right))

    def south(array):
        return pltpu.roll(array, 1, 1)

    def north(array):
        return pltpu.roll(array, width - 1, 1)

    for t in range(ahead):
        source = (chunk * steps + pl.program_id(0)) * sources + t // pairs
        lanes = slice(t % pairs * width, (t % pairs + 1) * width)

        def around(kind, first):
            faces = [
                winds[source, 0, kind, 1:2, lanes],
                winds[source, 1, kind, 0:2, lanes],
                winds[source, 2, kind, 0:2, lanes],
            ]
            return jnp.concatenate(faces, axis=0)[first : first + 4]

        east = around(0, 0)
        east_next = around(0, 1)
        upward = around(1, 0)
        upward_next = jnp.where(y == NY - 1, 0.0, north(upward))
        upward = jnp.where(y == 0, 0.0, upward)
        here = (
            1.0
            + jnp.minimum(east, 0.0)
            - jnp.maximum(east_next, 0.0)
            + jnp.minimum(upward, 0.0)
            - jnp.maximum(upward_next, 0.0)
        )
        west_of = jnp.maximum(east, 0.0)
        east_of = -jnp.minimum(east_next, 0.0)
        south_of = jnp.maximum(upward, 0.0)
        north_of = -jnp.minimum(upward_next, 0.0)

        def step(q, at, west, east):
            row = slice(at, at + 1)
            return (
                here[row] * q
                + west_of[row] * west
                + east_of[row] * east
                + south_of[row] * south(q)
                + north_of[row] * north(q)
            )

        for first in range(0, count, rows):

            def column(ref, c):
                start = first * stride + 2 * pieces * t + c
                return jnp.concatenate(
                    [ref[pl.ds(start + 2 * m, rows, stride=stride), :] for m in range(pieces)], axis=1
                )

            q = [column(ref, c) for ref in (left, own, right) for c in range(2)]
            q = [step(q[i + 1], i, q[i], q[i + 2]) for i in range(4)]
            for c in range(2):
                out[t, first : first + rows, c * width : (c + 1) * width] = step(
                    q[c + 1], c + 1, q[c], q[c + 2]
                )


def transport(chunk, winds, left, own, right, shape):
    groups, count, twice = shape
    steps = 2
    sides = [array.reshape(count, -1, LANES) for array in (left, own, right)]
    part = sides[0].shape[1] // steps
    return pl.pallas_call(
        functools.partial(transport_kernel, chunk),
        grid=(steps,),
        in_specs=[VMEM] + [pl.BlockSpec((count, part, LANES), lambda s: (0, s, 0))] * 3,
        out_specs=pl.BlockSpec((groups // steps, count, twice), lambda s: (s, 0, 0)),
        out_shape=pltpu.HBM(shape, F32),
        compiler_params=pltpu.CompilerParams(vmem_limit_bytes=16 << 20),
        name="transport",
    )(winds, *sides)


def join_kernel(y_ref, *refs):
    x_ref = refs[-1]
    groups, rows, twice = y_ref.shape
    width = twice // 2
    pieces = width // LANES
    stride = x_ref.shape[1]
    flat = x_ref.reshape(rows * stride, LANES)
    for t in range(groups):
        for c in range(2):
            for m in range(pieces):
                lane = c * width + m * LANES
                flat[pl.ds(2 * (t * pieces + m) + c, rows, stride=stride), :] = y_ref[t, :, lane : lane + LANES]


def join(blocks, so_far, chunk):
    groups, own, twice = blocks.shape
    length = groups * twice // LANES
    more = [] if so_far is None else [so_far]
    return pl.pallas_call(
        join_kernel,
        grid=(own // 8,),
        in_specs=[pl.BlockSpec((groups, 8, twice), lambda i: (0, i, 0))]
        + [pl.BlockSpec(memory_space=pl.ANY)] * len(more),
        out_specs=pl.BlockSpec((8, length, LANES), lambda i: (i, chunk, 0)),
        out_shape=jax.ShapeDtypeStruct((own, CHUNKS * length, LANES), F32),
        input_output_aliases={1: 0} if more else {},
        name="join",
    )(blocks, *more)


def split(values):
    high = values.astype(BF16)
    low = (values - high.astype(F32)).astype(BF16)
    return jnp.concatenate([high, low], axis=0)


def react_kernel(cells, pick1, pick2, change, rates, out):
    amounts = cells[...]
    rate = jnp.concatenate(
        [jnp.broadcast_to(rates[i : i + 1, :], (LANES, LANES)).T for i in range(rates.shape[0])], axis=0
    )
    rate = jnp.concatenate([rate] * (amounts.shape[1] // LANES), axis=1)
    for step in range(SUBSTEPS):
        parts = split(amounts)
        first = jnp.dot(pick1[...], parts, preferred_element_type=F32)
        second = jnp.dot(pick2[...], parts, preferred_element_type=F32)
        velocity = split(rate * first * second)
        amounts = amounts + jnp.dot(change[...], velocity, preferred_element_type=F32)
    out[...] = amounts


def react(cells, pick1, pick2, change, rates):
    return pl.pallas_call(
        react_kernel,
        in_specs=[VMEM] * 5,
        out_specs=VMEM,
        out_shape=jax.ShapeDtypeStruct(cells.shape, F32),
        compiler_params=pltpu.CompilerParams(vmem_limit_bytes=24 << 20),
        name="react",
    )(cells, pick1, pick2, change, rates)


def neighbours(array):
    count = lax.axis_size("region")
    left = lax.ppermute(array, "region", [(i, (i + 1) % count) for i in range(count)])
    right = lax.ppermute(array, "region", [((i + 1) % count, i) for i in range(count)])
    return left, right


def tables(first_reactant, second_reactant, product_species, rate_coeff):
    species = jnp.arange(2 * TRACERS, dtype=jnp.int32) % TRACERS
    pick1 = (first_reactant[:, None] == species[None, :]).astype(BF16)
    pick2 = (second_reactant[:, None] == species[None, :]).astype(BF16)
    kinds = jnp.arange(TRACERS, dtype=jnp.int32)[:, None]
    change = (
        (product_species[None, :] == kinds).astype(F32)
        - (first_reactant[None, :] == kinds).astype(F32)
        - (second_reactant[None, :] == kinds).astype(F32)
    ).astype(BF16)
    change = jnp.concatenate([change, change], axis=1)
    return pick1, pick2, change, rate_coeff.reshape(-1, LANES)


def exchange(blocks):
    return lax.all_to_all(blocks, "tracer", split_axis=0, concat_axis=0, tiled=True)


def body(tracers, fluxes, rate_coeff, first_reactant, second_reactant, product_species):
    groups = lax.axis_size("tracer")
    count, cols, length = tracers.shape
    width = length // groups // CHUNKS

    part = length // CHUNKS
    before, after = neighbours(fluxes)
    own, sides = [], []
    for k in range(CHUNKS):
        raw = lax.slice_in_dim(tracers, k * part, (k + 1) * part, axis=2)
        raw, tracers = lax.optimization_barrier((raw, tracers))
        own.append(as_tiles(raw))
        sides.append(neighbours(own[k]))
    section = jnp.stack([before, fluxes, after])
    winds = exchange(jnp.broadcast_to(section, (groups, *section.shape)))
    table = tables(first_reactant, second_reactant, product_species, rate_coeff)
    winds, table = lax.optimization_barrier((winds, table))

    out = None
    for k in range(CHUNKS):
        left, right = sides[k]
        moved = transport(k, winds, left, own[k], right, (groups, count, cols * width))
        cells = exchange(moved).reshape(groups * count, cols * width)
        reacted = react(cells, *table)
        back = exchange(reacted.reshape(groups, count, cols * width))
        out = join(back, out, k)
    return from_tiles(out, (count, cols, length))


def solution(mesh):
    in_specs = (P("tracer", "region", None), P(None, "region", "tracer"), P(), P(), P(), P())
    out_specs = P("tracer", "region", None)
    return jax.shard_map(body, mesh=mesh, in_specs=in_specs, out_specs=out_specs, check_vma=False)
```

```python
import functools

import jax
import jax.numpy as jnp
from jax import lax
from jax.experimental import pallas as pl
from jax.experimental.pallas import tpu as pltpu
from jax.sharding import Mesh, PartitionSpec as P

TRACERS = 256
NY = 48
SUBSTEPS = 4
LANES = 128
CHUNKS = 2
F32 = jnp.float32
BF16 = jnp.bfloat16
VMEM = pl.BlockSpec(memory_space=pltpu.VMEM)
PLANE = ("yhi", "tracer")
RING = ("z", "core")
REGION = ("yhi", "z", "core")


def low_half(shape):
    return lax.broadcasted_iota(jnp.int32, shape, 1) < LANES // 2


def turned(tile):
    return pltpu.roll(tile, LANES // 2, 1)


def to_blocks_kernel(chunk, x_ref, o_ref):
    rows = o_ref.shape[2]
    stride = x_ref.shape[0] // rows
    low = low_half((rows, LANES))

    def tile(j, c):
        return x_ref[pl.ds(2 * j + c, rows, stride=stride), :]

    for t in range(o_ref.shape[1]):
        j = (t * CHUNKS + chunk) * 3
        a0, a1, a2 = (tile(j + m, 0) for m in range(3))
        b0, b1, b2 = (tile(j + m, 1) for m in range(3))
        o_ref[0, t, :, 0:128] = a0
        o_ref[0, t, :, 128:256] = jnp.where(low, a1, turned(b0))
        o_ref[0, t, :, 256:384] = jnp.where(low, turned(b0), turned(b1))
        o_ref[1, t, :, 0:128] = jnp.where(low, turned(a1), turned(a2))
        o_ref[1, t, :, 128:256] = jnp.where(low, turned(a2), b1)
        o_ref[1, t, :, 256:384] = b2


def from_blocks_kernel(*refs):
    *y_refs, x_ref = refs
    rows = y_refs[0].shape[2]
    stride = x_ref.shape[0] // rows
    low = low_half((rows, LANES))

    def put(j, c, value):
        x_ref[pl.ds(2 * j + c, rows, stride=stride), :] = value

    for t in range(y_refs[0].shape[1]):
        for chunk, y_ref in enumerate(y_refs):
            j = (t * CHUNKS + chunk) * 3
            s0, s1, s2 = (y_ref[0, t, :, m * 128 : m * 128 + 128] for m in range(3))
            n0, n1, n2 = (y_ref[1, t, :, m * 128 : m * 128 + 128] for m in range(3))
            put(j, 0, s0)
            put(j + 1, 0, jnp.where(low, s1, turned(n0)))
            put(j + 2, 0, jnp.where(low, turned(n0), turned(n1)))
            put(j, 1, jnp.where(low, turned(s1), turned(s2)))
            put(j + 1, 1, jnp.where(low, turned(s2), n1))
            put(j + 2, 1, n2)


def to_blocks(tracers, chunk, groups):
    own, cols, length = tracers.shape
    width = length // groups // CHUNKS
    tiles = tracers.reshape(own, cols, length // LANES, LANES)
    tiles = jnp.transpose(tiles, (0, 2, 1, 3)).reshape(-1, LANES)
    steps = own // 8
    return pl.pallas_call(
        functools.partial(to_blocks_kernel, chunk),
        grid=(steps,),
        in_specs=[pl.BlockSpec((tiles.shape[0] // steps, LANES), lambda i: (i, 0))],
        out_specs=pl.BlockSpec((2, groups, 8, width), lambda i: (0, 0, i, 0)),
        out_shape=pltpu.HBM((2, groups, own, width), F32),
        name="to_blocks",
    )(tiles)


def from_blocks(blocks, shape):
    own, cols, length = shape
    _, groups, _, width = blocks[0].shape
    steps = own // 8
    rows = own * cols * length // LANES
    tiles = pl.pallas_call(
        from_blocks_kernel,
        grid=(steps,),
        in_specs=[pl.BlockSpec((2, groups, 8, width), lambda i: (0, 0, i, 0))] * CHUNKS,
        out_specs=pl.BlockSpec((rows // steps, LANES), lambda i: (i, 0)),
        out_shape=jax.ShapeDtypeStruct((rows, LANES), F32),
        name="from_blocks",
    )(*blocks)
    tiles = tiles.reshape(own, length // LANES, cols, LANES)
    return jnp.transpose(tiles, (0, 2, 1, 3)).reshape(shape)


def transport_kernel(swap, winds, own, left, right, cells):
    width = own.shape[2]
    col = width // 2
    rows = 32
    row = lax.rem(lax.broadcasted_iota(jnp.int32, (1, 4 * col), 1), NY)

    for h in range(2):
        from_left = jnp.where(swap[0] == 1, 1 - h, h)
        from_right = jnp.where(swap[1] == 1, 1 - h, h)
        u = winds[h, 0:1, col : 5 * col]
        u_next = winds[h, 0:1, 2 * col : 6 * col]
        v = jnp.where(row == 0, 0.0, winds[h, 1:2, col : 5 * col])
        v_next = jnp.where(row == NY - 1, 0.0, winds[h, 1:2, col + 1 : 5 * col + 1])
        here = (
            1.0
            + jnp.minimum(u, 0.0)
            - jnp.maximum(u_next, 0.0)
            + jnp.minimum(v, 0.0)
            - jnp.maximum(v_next, 0.0)
        )
        wide = [
            here,
            jnp.maximum(u, 0.0),
            -jnp.minimum(u_next, 0.0),
            jnp.maximum(v, 0.0),
            -jnp.minimum(v_next, 0.0),
        ]
        narrow = [array[:, col : 3 * col] for array in wide]

        def step(q, weights):
            n = weights[0].shape[1]
            shifts = (col, 0, 2 * col, col - 1, col + 1)
            terms = [w * q[:, s : s + n] for w, s in zip(weights, shifts)]
            return terms[0] + terms[1] + terms[2] + terms[3] + terms[4]

        for first in range(0, own.shape[1], rows):
            at = slice(first, first + rows)
            q = jnp.concatenate([left[from_left, at, :], own[h, at, :], right[from_right, at, :]], axis=1)
            cells[at, h * width : (h + 1) * width] = step(step(q, wide), narrow)


def transport(swap, winds, own, left, right):
    _, count, width = own.shape
    steps = 4
    part = pl.BlockSpec((2, count // steps, width), lambda i: (0, i, 0))
    return pl.pallas_call(
        transport_kernel,
        grid=(steps,),
        in_specs=[pl.BlockSpec(memory_space=pltpu.SMEM), VMEM, part, part, part],
        out_specs=pl.BlockSpec((count // steps, 2 * width), lambda i: (i, 0)),
        out_shape=jax.ShapeDtypeStruct((count, 2 * width), F32),
        compiler_params=pltpu.CompilerParams(vmem_limit_bytes=16 << 20),
        name="transport",
    )(swap, winds, own, left, right)


def split(values):
    high = values.astype(BF16)
    low = (values - high.astype(F32)).astype(BF16)
    return jnp.concatenate([high, low], axis=0)


def react_kernel(cells, pick1, pick2, change, rates, out):
    amounts = cells[...]
    rate = jnp.concatenate(
        [jnp.broadcast_to(rates[i : i + 1, :], (LANES, LANES)).T for i in range(rates.shape[0])], axis=0
    )
    rate = jnp.concatenate([rate] * (amounts.shape[1] // LANES), axis=1)
    for step in range(SUBSTEPS):
        parts = split(amounts)
        first = jnp.dot(pick1[...], parts, preferred_element_type=F32)
        second = jnp.dot(pick2[...], parts, preferred_element_type=F32)
        velocity = split(rate * first * second)
        amounts = amounts + jnp.dot(change[...], velocity, preferred_element_type=F32)
    width = out.shape[2]
    for h in range(2):
        out[h] = amounts[:, h * width : (h + 1) * width]


def react(cells, pick1, pick2, change, rates):
    return pl.pallas_call(
        react_kernel,
        in_specs=[VMEM] * 5,
        out_specs=VMEM,
        out_shape=jax.ShapeDtypeStruct((2, cells.shape[0], cells.shape[1] // 2), F32),
        compiler_params=pltpu.CompilerParams(vmem_limit_bytes=24 << 20),
        name="react",
    )(cells, pick1, pick2, change, rates)


def neighbours(array):
    count = lax.axis_size(RING)
    left = lax.ppermute(array, RING, [(i, (i + 1) % count) for i in range(count)])
    right = lax.ppermute(array, RING, [((i + 1) % count, i) for i in range(count)])
    return left, right


def all_winds(fluxes):
    regions = lax.axis_size(REGION)
    half = lax.axis_index("yhi")

    def from_region(ahead):
        if ahead == 0:
            return fluxes
        return lax.ppermute(fluxes, REGION, [((i + ahead) % regions, i) for i in range(regions)])

    def mine(array):
        array = array.reshape(2, array.shape[1], CHUNKS, 2, -1)
        return jnp.where(half == 0, array[:, :, :, 0], array[:, :, :, 1])

    own = [mine(from_region(d)) for d in (-1, 0, 1)]
    other = [mine(from_region(regions // 2 + d)) for d in (-1, 0, 1)]
    parts = []
    for h in range(2):
        trio = [jnp.where(half == h, a, b) for a, b in zip(own, other)]
        parts.append(jnp.stack(trio))
    winds = jnp.stack(parts)
    winds = jnp.transpose(winds, (0, 4, 2, 1, 3, 5))
    return winds.reshape(2, CHUNKS, 2, -1)


def tables(first_reactant, second_reactant, product_species, rate_coeff):
    species = jnp.arange(2 * TRACERS, dtype=jnp.int32) % TRACERS
    pick1 = (first_reactant[:, None] == species[None, :]).astype(BF16)
    pick2 = (second_reactant[:, None] == species[None, :]).astype(BF16)
    kinds = jnp.arange(TRACERS, dtype=jnp.int32)[:, None]
    change = (
        (product_species[None, :] == kinds).astype(F32)
        - (first_reactant[None, :] == kinds).astype(F32)
        - (second_reactant[None, :] == kinds).astype(F32)
    ).astype(BF16)
    change = jnp.concatenate([change, change], axis=1)
    return pick1, pick2, change, rate_coeff.reshape(-1, LANES)


def exchange(blocks):
    return lax.all_to_all(blocks, PLANE, split_axis=0, concat_axis=0, tiled=True)


def body(tracers, fluxes, rate_coeff, first_reactant, second_reactant, product_species):
    groups = lax.axis_size("tracer")
    own = tracers.shape[0]
    count = lax.axis_size(RING)
    place = lax.axis_index(RING)
    swap = jnp.stack([place == 0, place == count - 1]).astype(jnp.int32)

    gathered = []
    for chunk in range(CHUNKS):
        blocks = to_blocks(tracers, chunk, groups)
        if chunk == 0:
            blocks, first_reactant, second_reactant, product_species = lax.optimization_barrier(
                (blocks, first_reactant, second_reactant, product_species)
            )
        gathered.append(exchange(blocks.reshape(2 * groups, own, -1)))
    table = tables(first_reactant, second_reactant, product_species, rate_coeff)
    winds = all_winds(fluxes)

    returned = []
    for chunk in range(CHUNKS):
        part = gathered[chunk]
        shape = (2, TRACERS, part.shape[-1])
        left, right = neighbours(part)
        cells = transport(
            swap, winds[:, chunk], part.reshape(shape), left.reshape(shape), right.reshape(shape)
        )
        reacted = react(cells, *table)
        back = exchange(reacted.reshape(part.shape))
        returned.append(back.reshape(2, groups, own, -1))
    return from_blocks(returned, tracers.shape)


def solution(mesh):
    regions, groups = mesh.devices.shape
    torus = Mesh(mesh.devices.reshape(2, regions // 4, 2, groups), ("yhi", "z", "core", "tracer"))
    in_specs = (P("tracer", REGION, None), P(None, REGION, "tracer"), P(), P(), P(), P())
    out_specs = P("tracer", REGION, None)
    return jax.shard_map(body, mesh=torus, in_specs=in_specs, out_specs=out_specs, check_vma=False)
```

```python
import functools

import jax
import jax.numpy as jnp
from jax import lax
from jax.experimental import pallas as pl
from jax.experimental.pallas import tpu as pltpu
from jax.sharding import PartitionSpec as P

TRACERS = 256
NY = 48
SUBSTEPS = 4
LANES = 128
CHUNKS = 2
F32 = jnp.float32
BF16 = jnp.bfloat16
VMEM = pl.BlockSpec(memory_space=pltpu.VMEM)


def as_tiles(tracers):
    own, cols, length = tracers.shape
    tiles = tracers.reshape(own, cols, length // LANES, LANES)
    return jnp.transpose(tiles, (0, 2, 1, 3)).reshape(-1, LANES)


def from_tiles(tiles, shape):
    own, cols, length = shape
    tiles = tiles.reshape(own, length // LANES, cols, LANES)
    return jnp.transpose(tiles, (0, 2, 1, 3)).reshape(shape)


def transport_kernel(chunk, winds, left, own, right, out):
    ahead, count, twice = out.shape
    width = twice // 2
    pieces = width // LANES
    stride = own.shape[1]
    pairs = winds.shape[4] // width
    rows = 16
    y = lax.rem(lax.broadcasted_iota(jnp.int32, (4, width), 1), NY)
    steps = pl.num_programs(0)
    sources = ahead // pairs
    left, own, right = (ref.reshape(count * stride, LANES) for ref in (left, own, right))

    def south(array):
        return pltpu.roll(array, 1, 1)

    def north(array):
        return pltpu.roll(array, width - 1, 1)

    for t in range(ahead):
        source = (chunk * steps + pl.program_id(0)) * sources + t // pairs
        lanes = slice(t % pairs * width, (t % pairs + 1) * width)

        def around(kind, first):
            faces = [
                winds[source, 0, kind, 1:2, lanes],
                winds[source, 1, kind, 0:2, lanes],
                winds[source, 2, kind, 0:2, lanes],
            ]
            return jnp.concatenate(faces, axis=0)[first : first + 4]

        east = around(0, 0)
        east_next = around(0, 1)
        upward = around(1, 0)
        upward_next = jnp.where(y == NY - 1, 0.0, north(upward))
        upward = jnp.where(y == 0, 0.0, upward)
        here = (
            1.0
            + jnp.minimum(east, 0.0)
            - jnp.maximum(east_next, 0.0)
            + jnp.minimum(upward, 0.0)
            - jnp.maximum(upward_next, 0.0)
        )
        west_of = jnp.maximum(east, 0.0)
        east_of = -jnp.minimum(east_next, 0.0)
        south_of = jnp.maximum(upward, 0.0)
        north_of = -jnp.minimum(upward_next, 0.0)

        def step(q, at, west, east):
            row = slice(at, at + 1)
            return (
                here[row] * q
                + west_of[row] * west
                + east_of[row] * east
                + south_of[row] * south(q)
                + north_of[row] * north(q)
            )

        for first in range(0, count, rows):

            def column(ref, c):
                start = first * stride + 2 * pieces * t + c
                return jnp.concatenate(
                    [ref[pl.ds(start + 2 * m, rows, stride=stride), :] for m in range(pieces)], axis=1
                )

            q = [column(ref, c) for ref in (left, own, right) for c in range(2)]
            q = [step(q[i + 1], i, q[i], q[i + 2]) for i in range(4)]
            for c in range(2):
                out[t, first : first + rows, c * width : (c + 1) * width] = step(
                    q[c + 1], c + 1, q[c], q[c + 2]
                )


def transport(chunk, winds, left, own, right, shape):
    groups, count, twice = shape
    steps = 2
    sides = [array.reshape(count, -1, LANES) for array in (left, own, right)]
    part = sides[0].shape[1] // steps
    return pl.pallas_call(
        functools.partial(transport_kernel, chunk),
        grid=(steps,),
        in_specs=[VMEM] + [pl.BlockSpec((count, part, LANES), lambda s: (0, s, 0))] * 3,
        out_specs=pl.BlockSpec((groups // steps, count, twice), lambda s: (s, 0, 0)),
        out_shape=pltpu.HBM(shape, F32),
        compiler_params=pltpu.CompilerParams(vmem_limit_bytes=16 << 20),
        name="transport",
    )(winds, *sides)


def join_kernel(y_ref, *refs):
    x_ref = refs[-1]
    groups, _, twice = y_ref.shape
    rows = x_ref.shape[0]
    at = pl.ds(pl.multiple_of(pl.program_id(0) * rows, rows), rows)
    width = twice // 2
    pieces = width // LANES
    stride = x_ref.shape[1]
    flat = x_ref.reshape(rows * stride, LANES)
    for t in range(groups):
        for c in range(2):
            for m in range(pieces):
                lane = c * width + m * LANES
                flat[pl.ds(2 * (t * pieces + m) + c, rows, stride=stride), :] = y_ref[t, at, lane : lane + LANES]


def join(blocks, so_far, chunk):
    groups, own, twice = blocks.shape
    length = groups * twice // LANES
    more = [] if so_far is None else [so_far]
    return pl.pallas_call(
        join_kernel,
        grid=(own // 8,),
        in_specs=[VMEM]
        + [pl.BlockSpec(memory_space=pl.ANY)] * len(more),
        out_specs=pl.BlockSpec((8, length, LANES), lambda i: (i, chunk, 0)),
        out_shape=jax.ShapeDtypeStruct((own, CHUNKS * length, LANES), F32),
        input_output_aliases={1: 0} if more else {},
        name="join",
    )(pltpu.with_memory_space_constraint(blocks, pltpu.VMEM), *more)


def split(values):
    high = values.astype(BF16)
    low = (values - high.astype(F32)).astype(BF16)
    return jnp.concatenate([high, low], axis=0)


def react_kernel(cells, pick1, pick2, change, rates, out, done, sems):
    amounts = cells[...]
    rate = jnp.concatenate(
        [jnp.broadcast_to(rates[i : i + 1, :], (LANES, LANES)).T for i in range(rates.shape[0])], axis=0
    )
    rate = jnp.concatenate([rate] * (amounts.shape[1] // LANES), axis=1)
    tile = 256
    copies = []
    for step in range(SUBSTEPS):
        parts = split(amounts)
        first = jnp.dot(pick1[...], parts, preferred_element_type=F32)
        second = jnp.dot(pick2[...], parts, preferred_element_type=F32)
        velocity = split(rate * first * second)
        if step < SUBSTEPS - 1:
            amounts = amounts + jnp.dot(change[...], velocity, preferred_element_type=F32)
            continue
        for n in range(amounts.shape[1] // tile):
            lanes = slice(n * tile, (n + 1) * tile)
            moved = jnp.dot(change[...], velocity[:, lanes], preferred_element_type=F32)
            done[:, lanes] = amounts[:, lanes] + moved
            copies.append(pltpu.make_async_copy(done.at[:, lanes], out.at[:, lanes], sems.at[n]))
            copies[-1].start()
    for copy in copies:
        copy.wait()


def react(cells, pick1, pick2, change, rates):
    return pl.pallas_call(
        react_kernel,
        in_specs=[VMEM] * 5,
        out_specs=pl.BlockSpec(memory_space=pltpu.HBM),
        out_shape=pltpu.HBM(cells.shape, F32),
        scratch_shapes=[pltpu.VMEM(cells.shape, F32), pltpu.SemaphoreType.DMA((cells.shape[1] // 256,))],
        compiler_params=pltpu.CompilerParams(vmem_limit_bytes=24 << 20),
        name="react",
    )(pltpu.with_memory_space_constraint(cells, pltpu.VMEM), pick1, pick2, change, rates)


def neighbours(array):
    count = lax.axis_size("region")
    left = lax.ppermute(array, "region", [(i, (i + 1) % count) for i in range(count)])
    right = lax.ppermute(array, "region", [((i + 1) % count, i) for i in range(count)])
    return left, right


def tables(first_reactant, second_reactant, product_species, rate_coeff):
    species = jnp.arange(2 * TRACERS, dtype=jnp.int32) % TRACERS
    pick1 = (first_reactant[:, None] == species[None, :]).astype(BF16)
    pick2 = (second_reactant[:, None] == species[None, :]).astype(BF16)
    kinds = jnp.arange(TRACERS, dtype=jnp.int32)[:, None]
    change = (
        (product_species[None, :] == kinds).astype(F32)
        - (first_reactant[None, :] == kinds).astype(F32)
        - (second_reactant[None, :] == kinds).astype(F32)
    ).astype(BF16)
    change = jnp.concatenate([change, change], axis=1)
    return pick1, pick2, change, rate_coeff.reshape(-1, LANES)


def exchange(blocks):
    return lax.all_to_all(blocks, "tracer", split_axis=0, concat_axis=0, tiled=True)


def body(tracers, fluxes, rate_coeff, first_reactant, second_reactant, product_species):
    groups = lax.axis_size("tracer")
    count, cols, length = tracers.shape
    width = length // groups // CHUNKS

    part = length // CHUNKS
    before, after = neighbours(fluxes)
    section = jnp.stack([before, fluxes, after])
    winds = exchange(jnp.broadcast_to(section, (groups, *section.shape)))
    own, sides = [], []
    for k in range(CHUNKS):
        raw = lax.slice_in_dim(tracers, k * part, (k + 1) * part, axis=2)
        raw, tracers = lax.optimization_barrier((raw, tracers))
        own.append(as_tiles(raw))
        if k > 0:
            own[k], winds = lax.optimization_barrier((own[k], winds))
        sides.append(neighbours(own[k]))
    table = tables(first_reactant, second_reactant, product_species, rate_coeff)
    winds, table = lax.optimization_barrier((winds, table))

    out = None
    for k in range(CHUNKS):
        left, right = sides[k]
        moved = transport(k, winds, left, own[k], right, (groups, count, cols * width))
        cells = exchange(moved).reshape(groups * count, cols * width)
        reacted = react(cells, *table)
        back = exchange(reacted.reshape(groups, count, cols * width))
        out = join(back, out, k)
    return from_tiles(out, (count, cols, length))


def solution(mesh):
    in_specs = (P("tracer", "region", None), P(None, "region", "tracer"), P(), P(), P(), P())
    out_specs = P("tracer", "region", None)
    return jax.shard_map(body, mesh=mesh, in_specs=in_specs, out_specs=out_specs, check_vma=False)
```

```python
import functools

import jax
import jax.numpy as jnp
from jax import lax
from jax.experimental import pallas as pl
from jax.experimental.pallas import tpu as pltpu
from jax.sharding import PartitionSpec as P

TRACERS = 256
NY = 48
SUBSTEPS = 4
LANES = 128
CHUNKS = 2
F32 = jnp.float32
BF16 = jnp.bfloat16
VMEM = pl.BlockSpec(memory_space=pltpu.VMEM)


def as_tiles(tracers):
    own, cols, length = tracers.shape
    tiles = tracers.reshape(own, cols, length // LANES, LANES)
    return jnp.transpose(tiles, (0, 2, 1, 3)).reshape(-1, LANES)


def from_tiles(tiles, shape):
    own, cols, length = shape
    tiles = tiles.reshape(own, length // LANES, cols, LANES)
    return jnp.transpose(tiles, (0, 2, 1, 3)).reshape(shape)


def transport_kernel(chunk, winds, left, own, right, out):
    ahead, count, twice = out.shape
    width = twice // 2
    pieces = width // LANES
    stride = own.shape[1]
    pairs = winds.shape[4] // width
    rows = 16
    y = lax.rem(lax.broadcasted_iota(jnp.int32, (4, width), 1), NY)
    steps = pl.num_programs(0)
    sources = ahead // pairs
    left, own, right = (ref.reshape(count * stride, LANES) for ref in (left, own, right))

    def south(array):
        return pltpu.roll(array, 1, 1)

    def north(array):
        return pltpu.roll(array, width - 1, 1)

    for t in range(ahead):
        source = (chunk * steps + pl.program_id(0)) * sources + t // pairs
        lanes = slice(t % pairs * width, (t % pairs + 1) * width)

        def around(kind, first):
            faces = [
                winds[source, 0, kind, 1:2, lanes],
                winds[source, 1, kind, 0:2, lanes],
                winds[source, 2, kind, 0:2, lanes],
            ]
            return jnp.concatenate(faces, axis=0)[first : first + 4]

        east = around(0, 0)
        east_next = around(0, 1)
        upward = around(1, 0)
        upward_next = jnp.where(y == NY - 1, 0.0, north(upward))
        upward = jnp.where(y == 0, 0.0, upward)
        here = (
            1.0
            + jnp.minimum(east, 0.0)
            - jnp.maximum(east_next, 0.0)
            + jnp.minimum(upward, 0.0)
            - jnp.maximum(upward_next, 0.0)
        )
        west_of = jnp.maximum(east, 0.0)
        east_of = -jnp.minimum(east_next, 0.0)
        south_of = jnp.maximum(upward, 0.0)
        north_of = -jnp.minimum(upward_next, 0.0)

        def step(q, at, west, east):
            row = slice(at, at + 1)
            return (
                here[row] * q
                + west_of[row] * west
                + east_of[row] * east
                + south_of[row] * south(q)
                + north_of[row] * north(q)
            )

        for first in range(0, count, rows):

            def column(ref, c):
                start = first * stride + 2 * pieces * t + c
                return jnp.concatenate(
                    [ref[pl.ds(start + 2 * m, rows, stride=stride), :] for m in range(pieces)], axis=1
                )

            q = [column(ref, c) for ref in (left, own, right) for c in range(2)]
            q = [step(q[i + 1], i, q[i], q[i + 2]) for i in range(4)]
            for c in range(2):
                out[t, first : first + rows, c * width : (c + 1) * width] = step(
                    q[c + 1], c + 1, q[c], q[c + 2]
                )


def transport(chunk, winds, left, own, right, shape):
    groups, count, twice = shape
    steps = 2
    sides = [array.reshape(count, -1, LANES) for array in (left, own, right)]
    part = sides[0].shape[1] // steps
    return pl.pallas_call(
        functools.partial(transport_kernel, chunk),
        grid=(steps,),
        in_specs=[VMEM] + [pl.BlockSpec((count, part, LANES), lambda s: (0, s, 0))] * 3,
        out_specs=pl.BlockSpec((groups // steps, count, twice), lambda s: (s, 0, 0)),
        out_shape=pltpu.HBM(shape, F32),
        compiler_params=pltpu.CompilerParams(vmem_limit_bytes=16 << 20),
        name="transport",
    )(winds, *sides)


def join_kernel(y_ref, *refs):
    x_ref = refs[-1]
    groups, _, twice = y_ref.shape
    rows = x_ref.shape[0]
    at = pl.ds(pl.multiple_of(pl.program_id(0) * rows, rows), rows)
    width = twice // 2
    pieces = width // LANES
    stride = x_ref.shape[1]
    flat = x_ref.reshape(rows * stride, LANES)
    for t in range(groups):
        for c in range(2):
            for m in range(pieces):
                lane = c * width + m * LANES
                flat[pl.ds(2 * (t * pieces + m) + c, rows, stride=stride), :] = y_ref[t, at, lane : lane + LANES]


def join(blocks, so_far, chunk):
    groups, own, twice = blocks.shape
    length = groups * twice // LANES
    more = [] if so_far is None else [so_far]
    return pl.pallas_call(
        join_kernel,
        grid=(own // 8,),
        in_specs=[VMEM]
        + [pl.BlockSpec(memory_space=pl.ANY)] * len(more),
        out_specs=pl.BlockSpec((8, length, LANES), lambda i: (i, chunk, 0)),
        out_shape=jax.ShapeDtypeStruct((own, CHUNKS * length, LANES), F32),
        input_output_aliases={1: 0} if more else {},
        name="join",
    )(pltpu.with_memory_space_constraint(blocks, pltpu.VMEM), *more)


def split(values):
    high = values.astype(BF16)
    low = (values - high.astype(F32)).astype(BF16)
    return jnp.concatenate([high, low], axis=0)


def react_kernel(cells, pick1, pick2, change, rates, out, done, sems):
    amounts = cells[...]
    rate = jnp.concatenate(
        [jnp.broadcast_to(rates[i : i + 1, :], (LANES, LANES)).T for i in range(rates.shape[0])], axis=0
    )
    rate = jnp.concatenate([rate] * (amounts.shape[1] // LANES), axis=1)
    tile = 256
    copies = []
    for step in range(SUBSTEPS):
        parts = split(amounts)
        first = jnp.dot(pick1[...], parts, preferred_element_type=F32)
        second = jnp.dot(pick2[...], parts, preferred_element_type=F32)
        velocity = split(rate * first * second)
        if step < SUBSTEPS - 1:
            amounts = amounts + jnp.dot(change[...], velocity, preferred_element_type=F32)
            continue
        for n in range(amounts.shape[1] // tile):
            lanes = slice(n * tile, (n + 1) * tile)
            moved = jnp.dot(change[...], velocity[:, lanes], preferred_element_type=F32)
            done[:, lanes] = amounts[:, lanes] + moved
            copies.append(pltpu.make_async_copy(done.at[:, lanes], out.at[:, lanes], sems.at[n]))
            copies[-1].start()
    for copy in copies:
        copy.wait()


def react(cells, pick1, pick2, change, rates):
    return pl.pallas_call(
        react_kernel,
        in_specs=[VMEM] * 5,
        out_specs=pl.BlockSpec(memory_space=pltpu.HBM),
        out_shape=pltpu.HBM(cells.shape, F32),
        scratch_shapes=[pltpu.VMEM(cells.shape, F32), pltpu.SemaphoreType.DMA((cells.shape[1] // 256,))],
        compiler_params=pltpu.CompilerParams(vmem_limit_bytes=24 << 20),
        name="react",
    )(pltpu.with_memory_space_constraint(cells, pltpu.VMEM), pick1, pick2, change, rates)


def neighbours(array):
    count = lax.axis_size("region")
    left = lax.ppermute(array, "region", [(i, (i + 1) % count) for i in range(count)])
    right = lax.ppermute(array, "region", [((i + 1) % count, i) for i in range(count)])
    return left, right


def tables(first_reactant, second_reactant, product_species, rate_coeff):
    species = jnp.arange(2 * TRACERS, dtype=jnp.int32) % TRACERS
    pick1 = (first_reactant[:, None] == species[None, :]).astype(BF16)
    pick2 = (second_reactant[:, None] == species[None, :]).astype(BF16)
    kinds = jnp.arange(TRACERS, dtype=jnp.int32)[:, None]
    first, second, product = (
        jnp.concatenate([array, array])[None, :] for array in (first_reactant, second_reactant, product_species)
    )
    change = (
        (product == kinds).astype(F32) - (first == kinds).astype(F32) - (second == kinds).astype(F32)
    ).astype(BF16)
    return pick1, pick2, change, rate_coeff.reshape(-1, LANES)


def exchange(blocks):
    return lax.all_to_all(blocks, "tracer", split_axis=0, concat_axis=0, tiled=True)


def body(tracers, fluxes, rate_coeff, first_reactant, second_reactant, product_species):
    groups = lax.axis_size("tracer")
    count, cols, length = tracers.shape
    width = length // groups // CHUNKS

    part = length // CHUNKS
    before, after = neighbours(fluxes)
    own, sides = [], []
    raw = lax.slice_in_dim(tracers, 0, part, axis=2)
    raw, tracers = lax.optimization_barrier((raw, tracers))
    own.append(as_tiles(raw))
    sides.append(neighbours(own[0]))
    section = jnp.stack([before, fluxes, after])
    copies = jnp.broadcast_to(section, (groups, *section.shape))
    copies, tracers, reactions = lax.optimization_barrier(
        (copies, tracers, (first_reactant, second_reactant, product_species))
    )
    winds = exchange(copies)
    table = tables(*reactions, rate_coeff)
    tracers, table = lax.optimization_barrier((tracers, table))
    raw = lax.slice_in_dim(tracers, part, 2 * part, axis=2)
    raw, winds, table = lax.optimization_barrier((raw, winds, table))
    own.append(as_tiles(raw))
    sides.append(neighbours(own[1]))

    out = None
    for k in range(CHUNKS):
        left, right = sides[k]
        moved = transport(k, winds, left, own[k], right, (groups, count, cols * width))
        cells = exchange(moved).reshape(groups * count, cols * width)
        reacted = react(cells, *table)
        back = exchange(reacted.reshape(groups, count, cols * width))
        out = join(back, out, k)
    return from_tiles(out, (count, cols, length))


def solution(mesh):
    in_specs = (P("tracer", "region", None), P(None, "region", "tracer"), P(), P(), P(), P())
    out_specs = P("tracer", "region", None)
    return jax.shard_map(body, mesh=mesh, in_specs=in_specs, out_specs=out_specs, check_vma=False)
```

```python
import functools

import jax
import jax.numpy as jnp
from jax import lax
from jax.experimental import pallas as pl
from jax.experimental.pallas import tpu as pltpu
from jax.sharding import PartitionSpec as P

TRACERS = 256
NY = 48
SUBSTEPS = 4
LANES = 128
CHUNKS = 2
F32 = jnp.float32
BF16 = jnp.bfloat16
VMEM = pl.BlockSpec(memory_space=pltpu.VMEM)


def as_tiles(tracers):
    own, cols, length = tracers.shape
    tiles = tracers.reshape(own, cols, length // LANES, LANES)
    return jnp.transpose(tiles, (0, 2, 1, 3)).reshape(-1, LANES)


def from_tiles(tiles, shape):
    own, cols, length = shape
    tiles = tiles.reshape(own, length // LANES, cols, LANES)
    return jnp.transpose(tiles, (0, 2, 1, 3)).reshape(shape)


def transport_kernel(chunk, winds, left, own, right, out):
    ahead, count, twice = out.shape
    width = twice // 2
    pieces = width // LANES
    stride = own.shape[1]
    pairs = winds.shape[4] // width
    rows = 16
    y = lax.rem(lax.broadcasted_iota(jnp.int32, (4, width), 1), NY)
    steps = pl.num_programs(0)
    sources = ahead // pairs
    left, own, right = (ref.reshape(count * stride, LANES) for ref in (left, own, right))

    def south(array):
        return pltpu.roll(array, 1, 1)

    def north(array):
        return pltpu.roll(array, width - 1, 1)

    for t in range(ahead):
        source = (chunk * steps + pl.program_id(0)) * sources + t // pairs
        lanes = slice(t % pairs * width, (t % pairs + 1) * width)

        def around(kind, first):
            faces = [
                winds[source, 0, kind, 1:2, lanes],
                winds[source, 1, kind, 0:2, lanes],
                winds[source, 2, kind, 0:2, lanes],
            ]
            return jnp.concatenate(faces, axis=0)[first : first + 4]

        east = around(0, 0)
        east_next = around(0, 1)
        upward = around(1, 0)
        upward_next = jnp.where(y == NY - 1, 0.0, north(upward))
        upward = jnp.where(y == 0, 0.0, upward)
        here = (
            1.0
            + jnp.minimum(east, 0.0)
            - jnp.maximum(east_next, 0.0)
            + jnp.minimum(upward, 0.0)
            - jnp.maximum(upward_next, 0.0)
        )
        west_of = jnp.maximum(east, 0.0)
        east_of = -jnp.minimum(east_next, 0.0)
        south_of = jnp.maximum(upward, 0.0)
        north_of = -jnp.minimum(upward_next, 0.0)

        def step(q, at, west, east):
            row = slice(at, at + 1)
            return (
                here[row] * q
                + west_of[row] * west
                + east_of[row] * east
                + south_of[row] * south(q)
                + north_of[row] * north(q)
            )

        for first in range(0, count, rows):

            def column(ref, c):
                start = first * stride + 2 * pieces * t + c
                return jnp.concatenate(
                    [ref[pl.ds(start + 2 * m, rows, stride=stride), :] for m in range(pieces)], axis=1
                )

            q = [column(ref, c) for ref in (left, own, right) for c in range(2)]
            q = [step(q[i + 1], i, q[i], q[i + 2]) for i in range(4)]
            for c in range(2):
                out[t, first : first + rows, c * width : (c + 1) * width] = step(
                    q[c + 1], c + 1, q[c], q[c + 2]
                )


def transport(chunk, winds, left, own, right, shape):
    groups, count, twice = shape
    steps = 2
    sides = [array.reshape(count, -1, LANES) for array in (left, own, right)]
    part = sides[0].shape[1] // steps
    return pl.pallas_call(
        functools.partial(transport_kernel, chunk),
        grid=(steps,),
        in_specs=[VMEM] + [pl.BlockSpec((count, part, LANES), lambda s: (0, s, 0))] * 3,
        out_specs=pl.BlockSpec((groups // steps, count, twice), lambda s: (s, 0, 0)),
        out_shape=pltpu.HBM(shape, F32),
        compiler_params=pltpu.CompilerParams(vmem_limit_bytes=16 << 20),
        name="transport",
    )(winds, *sides)


def join_kernel(y_ref, *refs):
    x_ref = refs[-1]
    groups, _, twice = y_ref.shape
    rows = x_ref.shape[0]
    at = pl.ds(pl.multiple_of(pl.program_id(0) * rows, rows), rows)
    width = twice // 2
    pieces = width // LANES
    stride = x_ref.shape[1]
    flat = x_ref.reshape(rows * stride, LANES)
    for t in range(groups):
        for c in range(2):
            for m in range(pieces):
                lane = c * width + m * LANES
                flat[pl.ds(2 * (t * pieces + m) + c, rows, stride=stride), :] = y_ref[t, at, lane : lane + LANES]


def join(blocks, so_far, chunk):
    groups, own, twice = blocks.shape
    length = groups * twice // LANES
    more = [] if so_far is None else [so_far]
    return pl.pallas_call(
        join_kernel,
        grid=(own // 8,),
        in_specs=[VMEM]
        + [pl.BlockSpec(memory_space=pl.ANY)] * len(more),
        out_specs=pl.BlockSpec((8, length, LANES), lambda i: (i, chunk, 0)),
        out_shape=jax.ShapeDtypeStruct((own, CHUNKS * length, LANES), F32),
        input_output_aliases={1: 0} if more else {},
        name="join",
    )(pltpu.with_memory_space_constraint(blocks, pltpu.VMEM), *more)


def split(values):
    high = values.astype(BF16)
    low = (values - high.astype(F32)).astype(BF16)
    return jnp.concatenate([high, low], axis=0)


def react_kernel(cells, pick1, pick2, change, rates, out, done, sems):
    amounts = cells[...]
    rate = jnp.concatenate(
        [jnp.broadcast_to(rates[i : i + 1, :], (LANES, LANES)).T for i in range(rates.shape[0])], axis=0
    )
    rate = jnp.concatenate([rate] * (amounts.shape[1] // LANES), axis=1)
    tile = 256
    copies = []
    for step in range(SUBSTEPS):
        parts = split(amounts)
        first = jnp.dot(pick1[...], parts, preferred_element_type=F32)
        second = jnp.dot(pick2[...], parts, preferred_element_type=F32)
        velocity = split(rate * first * second)
        if step < SUBSTEPS - 1:
            amounts = amounts + jnp.dot(change[...], velocity, preferred_element_type=F32)
            continue
        for n in range(amounts.shape[1] // tile):
            lanes = slice(n * tile, (n + 1) * tile)
            moved = jnp.dot(change[...], velocity[:, lanes], preferred_element_type=F32)
            done[:, lanes] = amounts[:, lanes] + moved
            copies.append(pltpu.make_async_copy(done.at[:, lanes], out.at[:, lanes], sems.at[n]))
            copies[-1].start()
    for copy in copies:
        copy.wait()


def react(cells, pick1, pick2, change, rates):
    return pl.pallas_call(
        react_kernel,
        in_specs=[VMEM] * 5,
        out_specs=pl.BlockSpec(memory_space=pltpu.HBM),
        out_shape=pltpu.HBM(cells.shape, F32),
        scratch_shapes=[pltpu.VMEM(cells.shape, F32), pltpu.SemaphoreType.DMA((cells.shape[1] // 256,))],
        compiler_params=pltpu.CompilerParams(vmem_limit_bytes=24 << 20),
        name="react",
    )(pltpu.with_memory_space_constraint(cells, pltpu.VMEM), pick1, pick2, change, rates)


def neighbours(array):
    count = lax.axis_size("region")
    left = lax.ppermute(array, "region", [(i, (i + 1) % count) for i in range(count)])
    right = lax.ppermute(array, "region", [((i + 1) % count, i) for i in range(count)])
    return left, right


def tables(first_reactant, second_reactant, product_species, rate_coeff):
    species = jnp.arange(2 * TRACERS, dtype=jnp.int32) % TRACERS
    pick1 = (first_reactant[:, None] == species[None, :]).astype(BF16)
    pick2 = (second_reactant[:, None] == species[None, :]).astype(BF16)
    kinds = jnp.arange(TRACERS, dtype=jnp.int32)[:, None]
    first, second, product = (
        jnp.concatenate([array, array])[None, :] for array in (first_reactant, second_reactant, product_species)
    )
    change = (
        (product == kinds).astype(F32) - (first == kinds).astype(F32) - (second == kinds).astype(F32)
    ).astype(BF16)
    return pick1, pick2, change, rate_coeff.reshape(-1, LANES)


def exchange(blocks):
    return lax.all_to_all(blocks, "tracer", split_axis=0, concat_axis=0, tiled=True)


def body(tracers, fluxes, rate_coeff, first_reactant, second_reactant, product_species):
    groups = lax.axis_size("tracer")
    count, cols, length = tracers.shape
    width = length // groups // CHUNKS

    part = length // CHUNKS
    before, after = neighbours(fluxes)
    own, sides = [], []
    raw = lax.slice_in_dim(tracers, 0, part, axis=2)
    raw, tracers = lax.optimization_barrier((raw, tracers))
    own.append(as_tiles(raw))
    sides.append(neighbours(own[0]))
    section = jnp.stack([before, fluxes, after])
    copies = jnp.broadcast_to(section, (groups, *section.shape))
    copies, tracers, reactions = lax.optimization_barrier(
        (copies, tracers, (first_reactant, second_reactant, product_species))
    )
    winds = exchange(copies)
    table = tables(*reactions, rate_coeff)
    tracers, table = lax.optimization_barrier((tracers, table))
    raw = lax.slice_in_dim(tracers, part, 2 * part, axis=2)
    raw, table = lax.optimization_barrier((raw, table))
    own.append(as_tiles(raw))
    sides.append(neighbours(own[1]))

    out = None
    for k in range(CHUNKS):
        left, right = sides[k]
        moved = transport(k, winds, left, own[k], right, (groups, count, cols * width))
        cells = exchange(moved).reshape(groups * count, cols * width)
        reacted = react(cells, *table)
        back = exchange(reacted.reshape(groups, count, cols * width))
        out = join(back, out, k)
    return from_tiles(out, (count, cols, length))


def solution(mesh):
    in_specs = (P("tracer", "region", None), P(None, "region", "tracer"), P(), P(), P(), P())
    out_specs = P("tracer", "region", None)
    return jax.shard_map(body, mesh=mesh, in_specs=in_specs, out_specs=out_specs, check_vma=False)
```

```python
import functools

import jax
import jax.numpy as jnp
from jax import lax
from jax.experimental import pallas as pl
from jax.experimental.pallas import tpu as pltpu
from jax.sharding import PartitionSpec as P

TRACERS = 256
NY = 48
SUBSTEPS = 4
LANES = 128
CHUNKS = 2
F32 = jnp.float32
BF16 = jnp.bfloat16
VMEM = pl.BlockSpec(memory_space=pltpu.VMEM)


def as_tiles(tracers):
    own, cols, length = tracers.shape
    tiles = tracers.reshape(own, cols, length // LANES, LANES)
    return jnp.transpose(tiles, (0, 2, 1, 3)).reshape(-1, LANES)


def from_tiles(tiles, shape):
    own, cols, length = shape
    tiles = tiles.reshape(own, length // LANES, cols, LANES)
    return jnp.transpose(tiles, (0, 2, 1, 3)).reshape(shape)


def transport_kernel(chunk, winds, left, own, right, out):
    ahead, count, twice = out.shape
    width = twice // 2
    pieces = width // LANES
    stride = own.shape[1]
    pairs = winds.shape[4] // width
    rows = 16
    y = lax.rem(lax.broadcasted_iota(jnp.int32, (4, width), 1), NY)
    steps = pl.num_programs(0)
    sources = ahead // pairs
    left, own, right = (ref.reshape(count * stride, LANES) for ref in (left, own, right))

    def south(array):
        return pltpu.roll(array, 1, 1)

    def north(array):
        return pltpu.roll(array, width - 1, 1)

    for t in range(ahead):
        source = (chunk * steps + pl.program_id(0)) * sources + t // pairs
        lanes = slice(t % pairs * width, (t % pairs + 1) * width)

        def around(kind, first):
            faces = [
                winds[source, 0, kind, 1:2, lanes],
                winds[source, 1, kind, 0:2, lanes],
                winds[source, 2, kind, 0:2, lanes],
            ]
            return jnp.concatenate(faces, axis=0)[first : first + 4]

        east = around(0, 0)
        east_next = around(0, 1)
        upward = around(1, 0)
        upward_next = jnp.where(y == NY - 1, 0.0, north(upward))
        upward = jnp.where(y == 0, 0.0, upward)
        here = (
            1.0
            + jnp.minimum(east, 0.0)
            - jnp.maximum(east_next, 0.0)
            + jnp.minimum(upward, 0.0)
            - jnp.maximum(upward_next, 0.0)
        )
        west_of = jnp.maximum(east, 0.0)
        east_of = -jnp.minimum(east_next, 0.0)
        south_of = jnp.maximum(upward, 0.0)
        north_of = -jnp.minimum(upward_next, 0.0)

        def step(q, at, west, east):
            row = slice(at, at + 1)
            return (
                here[row] * q
                + west_of[row] * west
                + east_of[row] * east
                + south_of[row] * south(q)
                + north_of[row] * north(q)
            )

        for first in range(0, count, rows):

            def column(ref, c):
                start = first * stride + 2 * pieces * t + c
                return jnp.concatenate(
                    [ref[pl.ds(start + 2 * m, rows, stride=stride), :] for m in range(pieces)], axis=1
                )

            q = [column(ref, c) for ref in (left, own, right) for c in range(2)]
            q = [step(q[i + 1], i, q[i], q[i + 2]) for i in range(4)]
            for c in range(2):
                out[t, first : first + rows, c * width : (c + 1) * width] = step(
                    q[c + 1], c + 1, q[c], q[c + 2]
                )


def transport(chunk, winds, left, own, right, shape):
    groups, count, twice = shape
    steps = 2
    sides = [array.reshape(count, -1, LANES) for array in (left, own, right)]
    part = sides[0].shape[1] // steps
    return pl.pallas_call(
        functools.partial(transport_kernel, chunk),
        grid=(steps,),
        in_specs=[VMEM] + [pl.BlockSpec((count, part, LANES), lambda s: (0, s, 0))] * 3,
        out_specs=pl.BlockSpec((groups // steps, count, twice), lambda s: (s, 0, 0)),
        out_shape=pltpu.HBM(shape, F32),
        compiler_params=pltpu.CompilerParams(vmem_limit_bytes=16 << 20),
        name="transport",
    )(winds, *sides)


def join_kernel(y_ref, *refs):
    x_ref = refs[-1]
    groups, _, twice = y_ref.shape
    rows = x_ref.shape[0]
    at = pl.ds(pl.multiple_of(pl.program_id(0) * rows, rows), rows)
    width = twice // 2
    pieces = width // LANES
    stride = x_ref.shape[1]
    flat = x_ref.reshape(rows * stride, LANES)
    for t in range(groups):
        for c in range(2):
            for m in range(pieces):
                lane = c * width + m * LANES
                flat[pl.ds(2 * (t * pieces + m) + c, rows, stride=stride), :] = y_ref[t, at, lane : lane + LANES]


def join(blocks, so_far, chunk):
    groups, own, twice = blocks.shape
    length = groups * twice // LANES
    more = [] if so_far is None else [so_far]
    return pl.pallas_call(
        join_kernel,
        grid=(own // 8,),
        in_specs=[VMEM]
        + [pl.BlockSpec(memory_space=pl.ANY)] * len(more),
        out_specs=pl.BlockSpec((8, length, LANES), lambda i: (i, chunk, 0)),
        out_shape=jax.ShapeDtypeStruct((own, CHUNKS * length, LANES), F32),
        input_output_aliases={1: 0} if more else {},
        name="join",
    )(pltpu.with_memory_space_constraint(blocks, pltpu.VMEM), *more)


def split(values):
    high = values.astype(BF16)
    low = (values - high.astype(F32)).astype(BF16)
    return jnp.concatenate([high, low], axis=0)


def react_kernel(cells, pick1, pick2, change, rates, out, held, sems):
    tile = 256
    count = cells.shape[1] // tile
    rate = jnp.concatenate(
        [jnp.broadcast_to(rates[i : i + 1, :], (LANES, LANES)).T for i in range(rates.shape[0])], axis=0
    )
    rate = jnp.concatenate([rate] * (tile // LANES), axis=1)
    lanes = [slice(n * tile, (n + 1) * tile) for n in range(count)]
    loads = [pltpu.make_async_copy(cells.at[:, at], held.at[:, at], sems.at[0, n]) for n, at in enumerate(lanes)]
    stores = [pltpu.make_async_copy(held.at[:, at], out.at[:, at], sems.at[1, n]) for n, at in enumerate(lanes)]
    for load in loads:
        load.start()
    amounts = [None] * count

    def finish(step, n, first, second):
        velocity = split(rate * first * second)
        amounts[n] = amounts[n] + jnp.dot(change[...], velocity, preferred_element_type=F32)
        if step == SUBSTEPS - 1:
            held[:, lanes[n]] = amounts[n]
            stores[n].start()

    pending = None
    for step in range(SUBSTEPS):
        for n in range(count):
            if step == 0:
                loads[n].wait()
                amounts[n] = held[:, lanes[n]]
            parts = split(amounts[n])
            first = jnp.dot(pick1[...], parts, preferred_element_type=F32)
            second = jnp.dot(pick2[...], parts, preferred_element_type=F32)
            if pending is not None:
                finish(*pending)
            pending = (step, n, first, second)
    finish(*pending)
    for store in stores:
        store.wait()


def react(cells, pick1, pick2, change, rates):
    return pl.pallas_call(
        react_kernel,
        in_specs=[pl.BlockSpec(memory_space=pl.ANY)] + [VMEM] * 4,
        out_specs=pl.BlockSpec(memory_space=pltpu.HBM),
        out_shape=pltpu.HBM(cells.shape, F32),
        scratch_shapes=[pltpu.VMEM(cells.shape, F32), pltpu.SemaphoreType.DMA((2, cells.shape[1] // 256))],
        compiler_params=pltpu.CompilerParams(vmem_limit_bytes=24 << 20),
        name="react",
    )(cells, pick1, pick2, change, rates)


def neighbours(array):
    count = lax.axis_size("region")
    left = lax.ppermute(array, "region", [(i, (i + 1) % count) for i in range(count)])
    right = lax.ppermute(array, "region", [((i + 1) % count, i) for i in range(count)])
    return left, right


def tables(first_reactant, second_reactant, product_species, rate_coeff):
    species = jnp.arange(2 * TRACERS, dtype=jnp.int32) % TRACERS
    pick1 = (first_reactant[:, None] == species[None, :]).astype(BF16)
    pick2 = (second_reactant[:, None] == species[None, :]).astype(BF16)
    kinds = jnp.arange(TRACERS, dtype=jnp.int32)[:, None]
    first, second, product = (
        jnp.concatenate([array, array])[None, :] for array in (first_reactant, second_reactant, product_species)
    )
    change = (
        (product == kinds).astype(F32) - (first == kinds).astype(F32) - (second == kinds).astype(F32)
    ).astype(BF16)
    return pick1, pick2, change, rate_coeff.reshape(-1, LANES)


def exchange(blocks):
    return lax.all_to_all(blocks, "tracer", split_axis=0, concat_axis=0, tiled=True)


def body(tracers, fluxes, rate_coeff, first_reactant, second_reactant, product_species):
    groups = lax.axis_size("tracer")
    count, cols, length = tracers.shape
    width = length // groups // CHUNKS

    part = length // CHUNKS
    before, after = neighbours(fluxes)
    own, sides = [], []
    raw = lax.slice_in_dim(tracers, 0, part, axis=2)
    raw, tracers = lax.optimization_barrier((raw, tracers))
    own.append(as_tiles(raw))
    sides.append(neighbours(own[0]))
    section = jnp.stack([before, fluxes, after])
    copies = jnp.broadcast_to(section, (groups, *section.shape))
    copies, tracers, reactions = lax.optimization_barrier(
        (copies, tracers, (first_reactant, second_reactant, product_species))
    )
    winds = exchange(copies)
    table = tables(*reactions, rate_coeff)
    tracers, table = lax.optimization_barrier((tracers, table))
    raw = lax.slice_in_dim(tracers, part, 2 * part, axis=2)
    raw, table = lax.optimization_barrier((raw, table))
    own.append(as_tiles(raw))
    sides.append(neighbours(own[1]))

    out = None
    for k in range(CHUNKS):
        left, right = sides[k]
        moved = transport(k, winds, left, own[k], right, (groups, count, cols * width))
        cells = exchange(moved).reshape(groups * count, cols * width)
        reacted = react(cells, *table)
        back = exchange(reacted.reshape(groups, count, cols * width))
        out = join(back, out, k)
    return from_tiles(out, (count, cols, length))


def solution(mesh):
    in_specs = (P("tracer", "region", None), P(None, "region", "tracer"), P(), P(), P(), P())
    out_specs = P("tracer", "region", None)
    return jax.shard_map(body, mesh=mesh, in_specs=in_specs, out_specs=out_specs, check_vma=False)
```

```python
import functools

import jax
import jax.numpy as jnp
from jax import lax
from jax.experimental import pallas as pl
from jax.experimental.pallas import tpu as pltpu
from jax.sharding import PartitionSpec as P

TRACERS = 256
NY = 48
SUBSTEPS = 4
LANES = 128
CHUNKS = 2
F32 = jnp.float32
BF16 = jnp.bfloat16
VMEM = pl.BlockSpec(memory_space=pltpu.VMEM)


def as_tiles(tracers):
    own, cols, length = tracers.shape
    tiles = tracers.reshape(own, cols, length // LANES, LANES)
    return jnp.transpose(tiles, (0, 2, 1, 3)).reshape(-1, LANES)


def from_tiles(tiles, shape):
    own, cols, length = shape
    tiles = tiles.reshape(own, length // LANES, cols, LANES)
    return jnp.transpose(tiles, (0, 2, 1, 3)).reshape(shape)


def transport_kernel(chunk, winds, left, own, right, out):
    groups, rows, twice = out.shape
    width = twice // 2
    pieces = width // LANES
    stride = own.shape[0] // rows
    pairs = winds.shape[4] // width
    y = lax.rem(lax.broadcasted_iota(jnp.int32, (4, width), 1), NY)

    def south(array):
        return pltpu.roll(array, 1, 1)

    def north(array):
        return pltpu.roll(array, width - 1, 1)

    for t in range(groups):
        source = chunk * (groups // pairs) + t // pairs
        lanes = slice(t % pairs * width, (t % pairs + 1) * width)

        def around(kind, first):
            faces = [
                winds[source, 0, kind, 1:2, lanes],
                winds[source, 1, kind, 0:2, lanes],
                winds[source, 2, kind, 0:2, lanes],
            ]
            return jnp.concatenate(faces, axis=0)[first : first + 4]

        east = around(0, 0)
        east_next = around(0, 1)
        upward = around(1, 0)
        upward_next = jnp.where(y == NY - 1, 0.0, north(upward))
        upward = jnp.where(y == 0, 0.0, upward)
        here = (
            1.0
            + jnp.minimum(east, 0.0)
            - jnp.maximum(east_next, 0.0)
            + jnp.minimum(upward, 0.0)
            - jnp.maximum(upward_next, 0.0)
        )
        west_of = jnp.maximum(east, 0.0)
        east_of = -jnp.minimum(east_next, 0.0)
        south_of = jnp.maximum(upward, 0.0)
        north_of = -jnp.minimum(upward_next, 0.0)

        def step(q, at, west, east):
            row = slice(at, at + 1)
            return (
                here[row] * q
                + west_of[row] * west
                + east_of[row] * east
                + south_of[row] * south(q)
                + north_of[row] * north(q)
            )

        def column(ref, c):
            start = 2 * pieces * t + c
            return jnp.concatenate(
                [ref[pl.ds(start + 2 * m, rows, stride=stride), :] for m in range(pieces)], axis=1
            )

        q = [column(ref, c) for ref in (left, own, right) for c in range(2)]
        q = [step(q[i + 1], i, q[i], q[i + 2]) for i in range(4)]
        for c in range(2):
            out[t, :, c * width : (c + 1) * width] = step(q[c + 1], c + 1, q[c], q[c + 2])


def transport(chunk, winds, left, own, right, shape):
    groups, count, twice = shape
    steps = count // 8
    part = own.shape[0] // steps
    return pl.pallas_call(
        functools.partial(transport_kernel, chunk),
        grid=(steps,),
        in_specs=[VMEM] + [pl.BlockSpec((part, LANES), lambda i: (i, 0))] * 3,
        out_specs=pl.BlockSpec((groups, 8, twice), lambda i: (0, i, 0)),
        out_shape=pltpu.HBM(shape, F32),
        compiler_params=pltpu.CompilerParams(vmem_limit_bytes=16 << 20),
        name="transport",
    )(winds, left, own, right)


def join_kernel(y_ref, *refs):
    x_ref = refs[-1]
    groups, _, twice = y_ref.shape
    rows = x_ref.shape[0]
    at = pl.ds(pl.multiple_of(pl.program_id(0) * rows, rows), rows)
    width = twice // 2
    pieces = width // LANES
    stride = x_ref.shape[1]
    flat = x_ref.reshape(rows * stride, LANES)
    for t in range(groups):
        for c in range(2):
            for m in range(pieces):
                lane = c * width + m * LANES
                flat[pl.ds(2 * (t * pieces + m) + c, rows, stride=stride), :] = y_ref[t, at, lane : lane + LANES]


def join(blocks, so_far, chunk):
    groups, own, twice = blocks.shape
    length = groups * twice // LANES
    more = [] if so_far is None else [so_far]
    return pl.pallas_call(
        join_kernel,
        grid=(own // 8,),
        in_specs=[VMEM]
        + [pl.BlockSpec(memory_space=pl.ANY)] * len(more),
        out_specs=pl.BlockSpec((8, length, LANES), lambda i: (i, chunk, 0)),
        out_shape=jax.ShapeDtypeStruct((own, CHUNKS * length, LANES), F32),
        input_output_aliases={1: 0} if more else {},
        name="join",
    )(pltpu.with_memory_space_constraint(blocks, pltpu.VMEM), *more)


def split(values):
    high = values.astype(BF16)
    low = (values - high.astype(F32)).astype(BF16)
    return jnp.concatenate([high, low], axis=0)


def react_kernel(cells, pick1, pick2, change, rates, out, held, done, sems):
    tile = 256
    lanes = [slice(n * tile, (n + 1) * tile) for n in range(cells.shape[1] // tile)]
    loads = [pltpu.make_async_copy(cells.at[:, at], held.at[:, at], sems.at[0, n]) for n, at in enumerate(lanes)]
    for load in loads:
        load.start()
    rate = jnp.concatenate(
        [jnp.broadcast_to(rates[i : i + 1, :], (LANES, LANES)).T for i in range(rates.shape[0])], axis=0
    )

    def velocity_of(amounts):
        parts = split(amounts)
        first = jnp.dot(pick1[...], parts, preferred_element_type=F32)
        second = jnp.dot(pick2[...], parts, preferred_element_type=F32)
        return split(jnp.concatenate([rate] * (amounts.shape[1] // LANES), axis=1) * first * second)

    pieces = []
    for load, at in zip(loads, lanes):
        load.wait()
        pieces.append(velocity_of(held[:, at]))
    velocity = jnp.concatenate(pieces, axis=1)
    amounts = held[...]
    for step in range(SUBSTEPS - 1):
        amounts = amounts + jnp.dot(change[...], velocity, preferred_element_type=F32)
        velocity = velocity_of(amounts)
    copies = []
    for n, at in enumerate(lanes):
        moved = jnp.dot(change[...], velocity[:, at], preferred_element_type=F32)
        done[:, at] = amounts[:, at] + moved
        copies.append(pltpu.make_async_copy(done.at[:, at], out.at[:, at], sems.at[1, n]))
        copies[-1].start()
    for copy in copies:
        copy.wait()


def react(cells, pick1, pick2, change, rates):
    return pl.pallas_call(
        react_kernel,
        in_specs=[pl.BlockSpec(memory_space=pl.ANY)] + [VMEM] * 4,
        out_specs=pl.BlockSpec(memory_space=pltpu.HBM),
        out_shape=pltpu.HBM(cells.shape, F32),
        scratch_shapes=[pltpu.VMEM(cells.shape, F32)] * 2 + [pltpu.SemaphoreType.DMA((2, cells.shape[1] // 256))],
        compiler_params=pltpu.CompilerParams(vmem_limit_bytes=24 << 20),
        name="react",
    )(cells, pick1, pick2, change, rates)


def neighbours(array):
    count = lax.axis_size("region")
    left = lax.ppermute(array, "region", [(i, (i + 1) % count) for i in range(count)])
    right = lax.ppermute(array, "region", [((i + 1) % count, i) for i in range(count)])
    return left, right


def tables(first_reactant, second_reactant, product_species, rate_coeff):
    species = jnp.arange(2 * TRACERS, dtype=jnp.int32) % TRACERS
    pick1 = (first_reactant[:, None] == species[None, :]).astype(BF16)
    pick2 = (second_reactant[:, None] == species[None, :]).astype(BF16)
    kinds = jnp.arange(TRACERS, dtype=jnp.int32)[:, None]
    first, second, product = (
        jnp.concatenate([array, array])[None, :] for array in (first_reactant, second_reactant, product_species)
    )
    change = (
        (product == kinds).astype(F32) - (first == kinds).astype(F32) - (second == kinds).astype(F32)
    ).astype(BF16)
    return pick1, pick2, change, rate_coeff.reshape(-1, LANES)


def exchange(blocks):
    return lax.all_to_all(blocks, "tracer", split_axis=0, concat_axis=0, tiled=True)


def body(tracers, fluxes, rate_coeff, first_reactant, second_reactant, product_species):
    groups = lax.axis_size("tracer")
    count, cols, length = tracers.shape
    width = length // groups // CHUNKS

    part = length // CHUNKS
    before, after = neighbours(fluxes)
    own, sides = [], []
    raw = lax.slice_in_dim(tracers, 0, part, axis=2)
    raw, tracers = lax.optimization_barrier((raw, tracers))
    own.append(as_tiles(raw))
    sides.append(neighbours(own[0]))
    section = jnp.stack([before, fluxes, after])
    copies = jnp.broadcast_to(section, (groups, *section.shape))
    copies, tracers, reactions = lax.optimization_barrier(
        (copies, tracers, (first_reactant, second_reactant, product_species))
    )
    winds = exchange(copies)
    table = tables(*reactions, rate_coeff)
    tracers, table = lax.optimization_barrier((tracers, table))
    raw = lax.slice_in_dim(tracers, part, 2 * part, axis=2)
    raw, table = lax.optimization_barrier((raw, table))
    own.append(as_tiles(raw))
    sides.append(neighbours(own[1]))

    out = None
    for k in range(CHUNKS):
        left, right = sides[k]
        moved = transport(k, winds, left, own[k], right, (groups, count, cols * width))
        cells = exchange(moved).reshape(groups * count, cols * width)
        reacted = react(cells, *table)
        back = exchange(reacted.reshape(groups, count, cols * width))
        out = join(back, out, k)
    return from_tiles(out, (count, cols, length))


def solution(mesh):
    in_specs = (P("tracer", "region", None), P(None, "region", "tracer"), P(), P(), P(), P())
    out_specs = P("tracer", "region", None)
    return jax.shard_map(body, mesh=mesh, in_specs=in_specs, out_specs=out_specs, check_vma=False)
```

```python
import functools

import jax
import jax.numpy as jnp
from jax import lax
from jax.experimental import pallas as pl
from jax.experimental.pallas import tpu as pltpu
from jax.sharding import PartitionSpec as P

TRACERS = 256
NY = 48
SUBSTEPS = 4
LANES = 128
CHUNKS = 2
F32 = jnp.float32
BF16 = jnp.bfloat16
VMEM = pl.BlockSpec(memory_space=pltpu.VMEM)


def as_tiles(tracers):
    own, cols, length = tracers.shape
    tiles = tracers.reshape(own, cols, length // LANES, LANES)
    return jnp.transpose(tiles, (0, 2, 1, 3)).reshape(-1, LANES)


def from_tiles(tiles, shape):
    own, cols, length = shape
    tiles = tiles.reshape(own, length // LANES, cols, LANES)
    return jnp.transpose(tiles, (0, 2, 1, 3)).reshape(shape)


def transport_kernel(chunk, winds, left, own, right, out):
    if chunk % 2 == 1:
        left, right = right, left
    ahead, count, twice = out.shape
    width = twice // 2
    pieces = width // LANES
    stride = own.shape[1]
    pairs = winds.shape[4] // width
    rows = 32
    y = lax.rem(lax.broadcasted_iota(jnp.int32, (4, width), 1), NY)
    steps = pl.num_programs(0)
    sources = ahead // pairs
    left, own, right = (ref.reshape(count * stride, LANES) for ref in (left, own, right))

    def south(array):
        return pltpu.roll(array, 1, 1)

    def north(array):
        return pltpu.roll(array, width - 1, 1)

    for t in range(ahead):
        source = (chunk * steps + pl.program_id(0)) * sources + t // pairs
        lanes = slice(t % pairs * width, (t % pairs + 1) * width)

        def around(kind, first):
            faces = [
                winds[source, 0, kind, 1:2, lanes],
                winds[source, 1, kind, 0:2, lanes],
                winds[source, 2, kind, 0:2, lanes],
            ]
            return jnp.concatenate(faces, axis=0)[first : first + 4]

        east = around(0, 0)
        east_next = around(0, 1)
        upward = around(1, 0)
        upward_next = jnp.where(y == NY - 1, 0.0, north(upward))
        upward = jnp.where(y == 0, 0.0, upward)
        here = (
            1.0
            + jnp.minimum(east, 0.0)
            - jnp.maximum(east_next, 0.0)
            + jnp.minimum(upward, 0.0)
            - jnp.maximum(upward_next, 0.0)
        )
        west_of = jnp.maximum(east, 0.0)
        east_of = -jnp.minimum(east_next, 0.0)
        south_of = jnp.maximum(upward, 0.0)
        north_of = -jnp.minimum(upward_next, 0.0)

        def step(q, at, west, east):
            row = slice(at, at + 1)
            return (
                here[row] * q
                + west_of[row] * west
                + east_of[row] * east
                + south_of[row] * south(q)
                + north_of[row] * north(q)
            )

        for first in range(0, count, rows):

            def column(ref, c):
                start = first * stride + 2 * pieces * t + c
                return jnp.concatenate(
                    [ref[pl.ds(start + 2 * m, rows, stride=stride), :] for m in range(pieces)], axis=1
                )

            q = [column(ref, c) for ref in (left, own, right) for c in range(2)]
            q = [step(q[i + 1], i, q[i], q[i + 2]) for i in range(4)]
            for c in range(2):
                out[t, first : first + rows, c * width : (c + 1) * width] = step(
                    q[c + 1], c + 1, q[c], q[c + 2]
                )


def transport(chunk, winds, left, own, right, shape):
    groups, count, twice = shape
    steps = 2
    sides = [array.reshape(count, -1, LANES) for array in ((right, own, left) if chunk % 2 == 1 else (left, own, right))]
    part = sides[0].shape[1] // steps
    return pl.pallas_call(
        functools.partial(transport_kernel, chunk),
        grid=(steps,),
        in_specs=[VMEM] + [pl.BlockSpec((count, part, LANES), lambda s: (0, s, 0))] * 3,
        out_specs=pl.BlockSpec((groups // steps, count, twice), lambda s: (s, 0, 0)),
        out_shape=pltpu.HBM(shape, F32),
        compiler_params=pltpu.CompilerParams(vmem_limit_bytes=16 << 20),
        name="transport",
    )(winds, *sides)


def join_kernel(y_ref, *refs):
    x_ref = refs[-1]
    groups, _, twice = y_ref.shape
    rows = x_ref.shape[0]
    at = pl.ds(pl.multiple_of(pl.program_id(0) * rows, rows), rows)
    width = twice // 2
    pieces = width // LANES
    stride = x_ref.shape[1]
    flat = x_ref.reshape(rows * stride, LANES)
    for t in range(groups):
        for c in range(2):
            for m in range(pieces):
                lane = c * width + m * LANES
                flat[pl.ds(2 * (t * pieces + m) + c, rows, stride=stride), :] = y_ref[t, at, lane : lane + LANES]


def join(blocks, so_far, chunk):
    groups, own, twice = blocks.shape
    length = groups * twice // LANES
    more = [] if so_far is None else [so_far]
    return pl.pallas_call(
        join_kernel,
        grid=(own // 8,),
        in_specs=[VMEM]
        + [pl.BlockSpec(memory_space=pl.ANY)] * len(more),
        out_specs=pl.BlockSpec((8, length, LANES), lambda i: (i, chunk, 0)),
        out_shape=jax.ShapeDtypeStruct((own, CHUNKS * length, LANES), F32),
        input_output_aliases={1: 0} if more else {},
        name="join",
    )(pltpu.with_memory_space_constraint(blocks, pltpu.VMEM), *more)


def split(values):
    high = values.astype(BF16)
    low = (values - high.astype(F32)).astype(BF16)
    return jnp.concatenate([high, low], axis=0)


def react_kernel(cells, pick1, pick2, change, rates, out, done, sems):
    amounts = cells[...]
    rate = jnp.concatenate(
        [jnp.broadcast_to(rates[i : i + 1, :], (LANES, LANES)).T for i in range(rates.shape[0])], axis=0
    )
    rate = jnp.concatenate([rate] * (amounts.shape[1] // LANES), axis=1)
    tile = 256
    copies = []
    for step in range(SUBSTEPS):
        parts = split(amounts)
        first = jnp.dot(pick1[...], parts, preferred_element_type=F32)
        second = jnp.dot(pick2[...], parts, preferred_element_type=F32)
        velocity = split(rate * first * second)
        if step < SUBSTEPS - 1:
            amounts = amounts + jnp.dot(change[...], velocity, preferred_element_type=F32)
            continue
        for n in range(amounts.shape[1] // tile):
            lanes = slice(n * tile, (n + 1) * tile)
            moved = jnp.dot(change[...], velocity[:, lanes], preferred_element_type=F32)
            done[:, lanes] = amounts[:, lanes] + moved
            copies.append(pltpu.make_async_copy(done.at[:, lanes], out.at[:, lanes], sems.at[n]))
            copies[-1].start()
    for copy in copies:
        copy.wait()


def react(cells, pick1, pick2, change, rates):
    return pl.pallas_call(
        react_kernel,
        in_specs=[VMEM] * 5,
        out_specs=pl.BlockSpec(memory_space=pltpu.HBM),
        out_shape=pltpu.HBM(cells.shape, F32),
        scratch_shapes=[pltpu.VMEM(cells.shape, F32), pltpu.SemaphoreType.DMA((cells.shape[1] // 256,))],
        compiler_params=pltpu.CompilerParams(vmem_limit_bytes=24 << 20),
        name="react",
    )(pltpu.with_memory_space_constraint(cells, pltpu.VMEM), pick1, pick2, change, rates)


def neighbours(array):
    count = lax.axis_size("region")
    left = lax.ppermute(array, "region", [(i, (i + 1) % count) for i in range(count)])
    right = lax.ppermute(array, "region", [((i + 1) % count, i) for i in range(count)])
    return left, right


def tables(first_reactant, second_reactant, product_species, rate_coeff):
    species = jnp.arange(2 * TRACERS, dtype=jnp.int32) % TRACERS
    pick1 = (first_reactant[:, None] == species[None, :]).astype(BF16)
    pick2 = (second_reactant[:, None] == species[None, :]).astype(BF16)
    kinds = jnp.arange(TRACERS, dtype=jnp.int32)[:, None]
    first, second, product = (
        jnp.concatenate([array, array])[None, :] for array in (first_reactant, second_reactant, product_species)
    )
    change = (
        (product == kinds).astype(F32) - (first == kinds).astype(F32) - (second == kinds).astype(F32)
    ).astype(BF16)
    return pick1, pick2, change, rate_coeff.reshape(-1, LANES)


def exchange(blocks):
    return lax.all_to_all(blocks, "tracer", split_axis=0, concat_axis=0, tiled=True)


def body(tracers, fluxes, rate_coeff, first_reactant, second_reactant, product_species):
    groups = lax.axis_size("tracer")
    count, cols, length = tracers.shape
    width = length // groups // CHUNKS

    part = length // CHUNKS
    before, after = neighbours(fluxes)
    own, sides = [], []
    raw = lax.slice_in_dim(tracers, 0, part, axis=2)
    raw, tracers = lax.optimization_barrier((raw, tracers))
    own.append(as_tiles(raw))
    sides.append(neighbours(own[0]))
    section = jnp.stack([before, fluxes, after])
    copies = jnp.broadcast_to(section, (groups, *section.shape))
    copies, tracers, reactions = lax.optimization_barrier(
        (copies, tracers, (first_reactant, second_reactant, product_species))
    )
    winds = exchange(copies)
    table = tables(*reactions, rate_coeff)
    tracers, table = lax.optimization_barrier((tracers, table))
    raw = lax.slice_in_dim(tracers, part, 2 * part, axis=2)
    raw, table = lax.optimization_barrier((raw, table))
    own.append(as_tiles(raw))
    sides.append(neighbours(own[1]))

    out = None
    for k in range(CHUNKS):
        left, right = sides[k]
        moved = transport(k, winds, left, own[k], right, (groups, count, cols * width))
        cells = exchange(moved).reshape(groups * count, cols * width)
        reacted = react(cells, *table)
        back = exchange(reacted.reshape(groups, count, cols * width))
        out = join(back, out, k)
    return from_tiles(out, (count, cols, length))


def solution(mesh):
    in_specs = (P("tracer", "region", None), P(None, "region", "tracer"), P(), P(), P(), P())
    out_specs = P("tracer", "region", None)
    return jax.shard_map(body, mesh=mesh, in_specs=in_specs, out_specs=out_specs, check_vma=False)
```

```python
import functools

import jax
import jax.numpy as jnp
from jax import lax
from jax.experimental import pallas as pl
from jax.experimental.pallas import tpu as pltpu
from jax.sharding import PartitionSpec as P

TRACERS = 256
NY = 48
SUBSTEPS = 4
LANES = 128
CHUNKS = 2
F32 = jnp.float32
BF16 = jnp.bfloat16
VMEM = pl.BlockSpec(memory_space=pltpu.VMEM)


def as_tiles(tracers):
    own, cols, length = tracers.shape
    tiles = tracers.reshape(own, cols, length // LANES, LANES)
    return jnp.transpose(tiles, (0, 2, 1, 3)).reshape(-1, LANES)


def from_tiles(tiles, shape):
    own, cols, length = shape
    tiles = tiles.reshape(own, length // LANES, cols, LANES)
    return jnp.transpose(tiles, (0, 2, 1, 3)).reshape(shape)


def transport_kernel(chunk, winds, left, own, right, out):
    ahead, count, twice = out.shape
    width = twice // 2
    pieces = width // LANES
    stride = own.shape[1]
    pairs = winds.shape[4] // width
    rows = 32
    y = lax.rem(lax.broadcasted_iota(jnp.int32, (4, width), 1), NY)
    steps = pl.num_programs(0)
    sources = ahead // pairs
    left, own, right = (ref.reshape(count * stride, LANES) for ref in (left, own, right))

    def south(array):
        return pltpu.roll(array, 1, 1)

    def north(array):
        return pltpu.roll(array, width - 1, 1)

    for t in range(ahead):
        source = (chunk * steps + pl.program_id(0)) * sources + t // pairs
        lanes = slice(t % pairs * width, (t % pairs + 1) * width)

        def around(kind, first):
            faces = [
                winds[source, 0, kind, 1:2, lanes],
                winds[source, 1, kind, 0:2, lanes],
                winds[source, 2, kind, 0:2, lanes],
            ]
            return jnp.concatenate(faces, axis=0)[first : first + 4]

        east = around(0, 0)
        east_next = around(0, 1)
        upward = around(1, 0)
        upward_next = jnp.where(y == NY - 1, 0.0, north(upward))
        upward = jnp.where(y == 0, 0.0, upward)
        here = (
            1.0
            + jnp.minimum(east, 0.0)
            - jnp.maximum(east_next, 0.0)
            + jnp.minimum(upward, 0.0)
            - jnp.maximum(upward_next, 0.0)
        )
        west_of = jnp.maximum(east, 0.0)
        east_of = -jnp.minimum(east_next, 0.0)
        south_of = jnp.maximum(upward, 0.0)
        north_of = -jnp.minimum(upward_next, 0.0)

        def step(q, at, west, east):
            row = slice(at, at + 1)
            return (
                here[row] * q
                + west_of[row] * west
                + east_of[row] * east
                + south_of[row] * south(q)
                + north_of[row] * north(q)
            )

        for first in range(0, count, rows):

            def column(ref, c):
                start = first * stride + 2 * pieces * t + c
                return jnp.concatenate(
                    [ref[pl.ds(start + 2 * m, rows, stride=stride), :] for m in range(pieces)], axis=1
                )

            q = [column(ref, c) for ref in (left, own, right) for c in range(2)]
            q = [step(q[i + 1], i, q[i], q[i + 2]) for i in range(4)]
            for c in range(2):
                out[t, first : first + rows, c * width : (c + 1) * width] = step(
                    q[c + 1], c + 1, q[c], q[c + 2]
                )


def transport(chunk, winds, left, own, right, shape):
    groups, count, twice = shape
    steps = 2
    sides = [array.reshape(count, -1, LANES) for array in (left, own, right)]
    part = sides[0].shape[1] // steps
    return pl.pallas_call(
        functools.partial(transport_kernel, chunk),
        grid=(steps,),
        in_specs=[VMEM] + [pl.BlockSpec((count, part, LANES), lambda s: (0, s, 0))] * 3,
        out_specs=pl.BlockSpec((groups // steps, count, twice), lambda s: (s, 0, 0)),
        out_shape=pltpu.HBM(shape, F32),
        compiler_params=pltpu.CompilerParams(vmem_limit_bytes=16 << 20),
        name="transport",
    )(winds, *sides)


def join_kernel(y_ref, *refs):
    x_ref = refs[-1]
    groups, _, twice = y_ref.shape
    rows = x_ref.shape[0]
    at = pl.ds(pl.multiple_of(pl.program_id(0) * rows, rows), rows)
    width = twice // 2
    pieces = width // LANES
    stride = x_ref.shape[1]
    flat = x_ref.reshape(rows * stride, LANES)
    for t in range(groups):
        for c in range(2):
            for m in range(pieces):
                lane = c * width + m * LANES
                flat[pl.ds(2 * (t * pieces + m) + c, rows, stride=stride), :] = y_ref[t, at, lane : lane + LANES]


def join(blocks, so_far, chunk):
    groups, own, twice = blocks.shape
    length = groups * twice // LANES
    more = [] if so_far is None else [so_far]
    return pl.pallas_call(
        join_kernel,
        grid=(own // 8,),
        in_specs=[VMEM]
        + [pl.BlockSpec(memory_space=pl.ANY)] * len(more),
        out_specs=pl.BlockSpec((8, length, LANES), lambda i: (i, chunk, 0)),
        out_shape=jax.ShapeDtypeStruct((own, CHUNKS * length, LANES), F32),
        input_output_aliases={1: 0} if more else {},
        name="join",
    )(pltpu.with_memory_space_constraint(blocks, pltpu.VMEM), *more)


def split(values):
    high = values.astype(BF16)
    low = (values - high.astype(F32)).astype(BF16)
    return jnp.concatenate([high, low], axis=0)


def react_kernel(cells, pick1, pick2, change, rates, out, done, sems):
    amounts = cells[...]
    rate = jnp.concatenate(
        [jnp.broadcast_to(rates[i : i + 1, :], (LANES, LANES)).T for i in range(rates.shape[0])], axis=0
    )
    rate = jnp.concatenate([rate] * (amounts.shape[1] // LANES), axis=1)
    tile = 256
    copies = []
    for step in range(SUBSTEPS):
        parts = split(amounts)
        first = jnp.dot(pick1[...], parts, preferred_element_type=F32)
        second = jnp.dot(pick2[...], parts, preferred_element_type=F32)
        velocity = split(rate * first * second)
        if step < SUBSTEPS - 1:
            amounts = amounts + jnp.dot(change[...], velocity, preferred_element_type=F32)
            continue
        for n in range(amounts.shape[1] // tile):
            lanes = slice(n * tile, (n + 1) * tile)
            moved = jnp.dot(change[...], velocity[:, lanes], preferred_element_type=F32)
            done[:, lanes] = amounts[:, lanes] + moved
            copies.append(pltpu.make_async_copy(done.at[:, lanes], out.at[:, lanes], sems.at[n]))
            copies[-1].start()
    for copy in copies:
        copy.wait()


def react(cells, pick1, pick2, change, rates):
    return pl.pallas_call(
        react_kernel,
        in_specs=[VMEM] * 5,
        out_specs=pl.BlockSpec(memory_space=pltpu.HBM),
        out_shape=pltpu.HBM(cells.shape, F32),
        scratch_shapes=[pltpu.VMEM(cells.shape, F32), pltpu.SemaphoreType.DMA((cells.shape[1] // 256,))],
        compiler_params=pltpu.CompilerParams(vmem_limit_bytes=24 << 20),
        name="react",
    )(pltpu.with_memory_space_constraint(cells, pltpu.VMEM), pick1, pick2, change, rates)


def neighbours(array):
    count = lax.axis_size("region")
    left = lax.ppermute(array, "region", [(i, (i + 1) % count) for i in range(count)])
    right = lax.ppermute(array, "region", [((i + 1) % count, i) for i in range(count)])
    return left, right


def tables(first_reactant, second_reactant, product_species, rate_coeff):
    species = jnp.arange(2 * TRACERS, dtype=jnp.int32) % TRACERS
    pick1 = (first_reactant[:, None] == species[None, :]).astype(BF16)
    pick2 = (second_reactant[:, None] == species[None, :]).astype(BF16)
    kinds = jnp.arange(TRACERS, dtype=jnp.int32)[:, None]
    first, second, product = (
        jnp.concatenate([array, array])[None, :] for array in (first_reactant, second_reactant, product_species)
    )
    change = (
        (product == kinds).astype(F32) - (first == kinds).astype(F32) - (second == kinds).astype(F32)
    ).astype(BF16)
    return pick1, pick2, change, rate_coeff.reshape(-1, LANES)


def exchange(blocks):
    return lax.all_to_all(blocks, "tracer", split_axis=0, concat_axis=0, tiled=True)


def body(tracers, fluxes, rate_coeff, first_reactant, second_reactant, product_species):
    groups = lax.axis_size("tracer")
    count, cols, length = tracers.shape
    width = length // groups // CHUNKS

    part = length // CHUNKS
    before, after = neighbours(fluxes)
    own, sides = [], []
    raw = lax.slice_in_dim(tracers, 0, part, axis=2)
    raw, tracers = lax.optimization_barrier((raw, tracers))
    own.append(as_tiles(raw))
    sides.append(neighbours(own[0]))
    section = jnp.stack([before, fluxes, after])
    copies = jnp.broadcast_to(section, (groups, *section.shape))
    copies, tracers, reactions = lax.optimization_barrier(
        (copies, tracers, (first_reactant, second_reactant, product_species))
    )
    winds = exchange(copies)
    table = tables(*reactions, rate_coeff)
    tracers, table = lax.optimization_barrier((tracers, table))
    raw = lax.slice_in_dim(tracers, part, 2 * part, axis=2)
    raw, table = lax.optimization_barrier((raw, table))
    own.append(as_tiles(raw))
    sides.append(neighbours(own[1]))

    out = None
    for k in range(CHUNKS):
        left, right = sides[k]
        moved = transport(k, winds, left, own[k], right, (groups, count, cols * width))
        cells = exchange(moved).reshape(groups * count, cols * width)
        reacted = react(cells, *table)
        back = exchange(reacted.reshape(groups, count, cols * width))
        out = join(back, out, k)
    return from_tiles(out, (count, cols, length))


def solution(mesh):
    in_specs = (P("tracer", "region", None), P(None, "region", "tracer"), P(), P(), P(), P())
    out_specs = P("tracer", "region", None)
    return jax.shard_map(body, mesh=mesh, in_specs=in_specs, out_specs=out_specs, check_vma=False)
```

```python
import functools

import jax
import jax.numpy as jnp
from jax import lax
from jax.experimental import pallas as pl
from jax.experimental.pallas import tpu as pltpu
from jax.sharding import PartitionSpec as P

TRACERS = 256
NY = 48
SUBSTEPS = 4
LANES = 128
CHUNKS = 2
F32 = jnp.float32
BF16 = jnp.bfloat16
VMEM = pl.BlockSpec(memory_space=pltpu.VMEM)


def as_tiles(tracers):
    own, cols, length = tracers.shape
    tiles = tracers.reshape(own, cols, length // LANES, LANES)
    return jnp.transpose(tiles, (0, 2, 1, 3)).reshape(-1, LANES)


def from_tiles(tiles, shape):
    own, cols, length = shape
    tiles = tiles.reshape(own, length // LANES, cols, LANES)
    return jnp.transpose(tiles, (0, 2, 1, 3)).reshape(shape)


def transport_kernel(chunk, winds, left, own, right, out):
    ahead, count, twice = out.shape
    width = twice // 2
    pieces = width // LANES
    stride = own.shape[1]
    pairs = winds.shape[4] // width
    rows = 32
    y = lax.rem(lax.broadcasted_iota(jnp.int32, (4, width), 1), NY)
    steps = pl.num_programs(0)
    sources = ahead // pairs
    left, own, right = (ref.reshape(count * stride, LANES) for ref in (left, own, right))

    def south(array):
        return pltpu.roll(array, 1, 1)

    def north(array):
        return pltpu.roll(array, width - 1, 1)

    for t in range(ahead):
        source = (chunk * steps + pl.program_id(0)) * sources + t // pairs
        lanes = slice(t % pairs * width, (t % pairs + 1) * width)

        def around(kind, first):
            faces = [
                winds[source, 0, kind, 1:2, lanes],
                winds[source, 1, kind, 0:2, lanes],
                winds[source, 2, kind, 0:2, lanes],
            ]
            return jnp.concatenate(faces, axis=0)[first : first + 4]

        east = around(0, 0)
        east_next = around(0, 1)
        upward = around(1, 0)
        upward_next = jnp.where(y == NY - 1, 0.0, north(upward))
        upward = jnp.where(y == 0, 0.0, upward)
        here = (
            1.0
            + jnp.minimum(east, 0.0)
            - jnp.maximum(east_next, 0.0)
            + jnp.minimum(upward, 0.0)
            - jnp.maximum(upward_next, 0.0)
        )
        west_of = jnp.maximum(east, 0.0)
        east_of = -jnp.minimum(east_next, 0.0)
        south_of = jnp.maximum(upward, 0.0)
        north_of = -jnp.minimum(upward_next, 0.0)

        def step(q, at, west, east):
            row = slice(at, at + 1)
            return (
                here[row] * q
                + west_of[row] * west
                + east_of[row] * east
                + south_of[row] * south(q)
                + north_of[row] * north(q)
            )

        for first in range(0, count, rows):

            def column(ref, c):
                start = first * stride + 2 * pieces * t + c
                return jnp.concatenate(
                    [ref[pl.ds(start + 2 * m, rows, stride=stride), :] for m in range(pieces)], axis=1
                )

            q = [column(ref, c) for ref in (left, own, right) for c in range(2)]
            q = [step(q[i + 1], i, q[i], q[i + 2]) for i in range(4)]
            for c in range(2):
                out[t, first : first + rows, c * width : (c + 1) * width] = step(
                    q[c + 1], c + 1, q[c], q[c + 2]
                )


def transport(chunk, winds, left, own, right, shape):
    groups, count, twice = shape
    steps = 2
    sides = [array.reshape(count, -1, LANES) for array in (left, own, right)]
    part = sides[0].shape[1] // steps
    return pl.pallas_call(
        functools.partial(transport_kernel, chunk),
        grid=(steps,),
        in_specs=[VMEM] + [pl.BlockSpec((count, part, LANES), lambda s: (0, s, 0))] * 3,
        out_specs=pl.BlockSpec((groups // steps, count, twice), lambda s: (s, 0, 0)),
        out_shape=pltpu.HBM(shape, F32),
        compiler_params=pltpu.CompilerParams(vmem_limit_bytes=16 << 20),
        name="transport",
    )(winds, *sides)


def join_kernel(y_ref, *refs):
    x_ref = refs[-1]
    groups, _, twice = y_ref.shape
    rows = x_ref.shape[0]
    at = pl.ds(pl.multiple_of(pl.program_id(0) * rows, rows), rows)
    width = twice // 2
    pieces = width // LANES
    stride = x_ref.shape[1]
    flat = x_ref.reshape(rows * stride, LANES)
    for t in range(groups):
        for c in range(2):
            for m in range(pieces):
                lane = c * width + m * LANES
                flat[pl.ds(2 * (t * pieces + m) + c, rows, stride=stride), :] = y_ref[t, at, lane : lane + LANES]


def join(blocks, so_far, chunk):
    groups, own, twice = blocks.shape
    length = groups * twice // LANES
    more = [] if so_far is None else [so_far]
    return pl.pallas_call(
        join_kernel,
        grid=(own // 8,),
        in_specs=[VMEM]
        + [pl.BlockSpec(memory_space=pl.ANY)] * len(more),
        out_specs=pl.BlockSpec((8, length, LANES), lambda i: (i, chunk, 0)),
        out_shape=jax.ShapeDtypeStruct((own, CHUNKS * length, LANES), F32),
        input_output_aliases={1: 0} if more else {},
        name="join",
    )(pltpu.with_memory_space_constraint(blocks, pltpu.VMEM), *more)


def split(values):
    high = values.astype(BF16)
    low = (values - high.astype(F32)).astype(BF16)
    return jnp.concatenate([high, low], axis=0)


def react_kernel(cells, pick1, pick2, change, rates, out, held, done, sems, load_sem):
    load = pltpu.make_async_copy(cells, held, load_sem)
    load.start()
    rate = jnp.concatenate(
        [jnp.broadcast_to(rates[i : i + 1, :], (LANES, LANES)).T for i in range(rates.shape[0])], axis=0
    )
    rate = jnp.concatenate([rate] * (cells.shape[1] // LANES), axis=1)
    load.wait()
    amounts = held[...]
    tile = 256
    copies = []
    for step in range(SUBSTEPS):
        parts = split(amounts)
        first = jnp.dot(pick1[...], parts, preferred_element_type=F32)
        second = jnp.dot(pick2[...], parts, preferred_element_type=F32)
        velocity = split(rate * first * second)
        if step < SUBSTEPS - 1:
            amounts = amounts + jnp.dot(change[...], velocity, preferred_element_type=F32)
            continue
        for n in range(amounts.shape[1] // tile):
            lanes = slice(n * tile, (n + 1) * tile)
            moved = jnp.dot(change[...], velocity[:, lanes], preferred_element_type=F32)
            done[:, lanes] = amounts[:, lanes] + moved
            copies.append(pltpu.make_async_copy(done.at[:, lanes], out.at[:, lanes], sems.at[n]))
            copies[-1].start()
    for copy in copies:
        copy.wait()


def react(cells, pick1, pick2, change, rates):
    return pl.pallas_call(
        react_kernel,
        in_specs=[pl.BlockSpec(memory_space=pl.ANY)] + [VMEM] * 4,
        out_specs=pl.BlockSpec(memory_space=pltpu.HBM),
        out_shape=pltpu.HBM(cells.shape, F32),
        scratch_shapes=[pltpu.VMEM(cells.shape, F32)] * 2
        + [pltpu.SemaphoreType.DMA((cells.shape[1] // 256,)), pltpu.SemaphoreType.DMA(())],
        compiler_params=pltpu.CompilerParams(vmem_limit_bytes=24 << 20),
        name="react",
    )(cells, pick1, pick2, change, rates)


def neighbours(array):
    count = lax.axis_size("region")
    left = lax.ppermute(array, "region", [(i, (i + 1) % count) for i in range(count)])
    right = lax.ppermute(array, "region", [((i + 1) % count, i) for i in range(count)])
    return left, right


def tables(first_reactant, second_reactant, product_species, rate_coeff):
    species = jnp.arange(2 * TRACERS, dtype=jnp.int32) % TRACERS
    pick1 = (first_reactant[:, None] == species[None, :]).astype(BF16)
    pick2 = (second_reactant[:, None] == species[None, :]).astype(BF16)
    kinds = jnp.arange(TRACERS, dtype=jnp.int32)[:, None]
    first, second, product = (
        jnp.concatenate([array, array])[None, :] for array in (first_reactant, second_reactant, product_species)
    )
    change = (
        (product == kinds).astype(F32) - (first == kinds).astype(F32) - (second == kinds).astype(F32)
    ).astype(BF16)
    return pick1, pick2, change, rate_coeff.reshape(-1, LANES)


def exchange(blocks):
    return lax.all_to_all(blocks, "tracer", split_axis=0, concat_axis=0, tiled=True)


def body(tracers, fluxes, rate_coeff, first_reactant, second_reactant, product_species):
    groups = lax.axis_size("tracer")
    count, cols, length = tracers.shape
    width = length // groups // CHUNKS

    part = length // CHUNKS
    before, after = neighbours(fluxes)
    own, sides = [], []
    raw = lax.slice_in_dim(tracers, 0, part, axis=2)
    raw, tracers = lax.optimization_barrier((raw, tracers))
    own.append(as_tiles(raw))
    sides.append(neighbours(own[0]))
    section = jnp.stack([before, fluxes, after])
    copies = jnp.broadcast_to(section, (groups, *section.shape))
    copies, tracers, reactions = lax.optimization_barrier(
        (copies, tracers, (first_reactant, second_reactant, product_species))
    )
    winds = exchange(copies)
    table = tables(*reactions, rate_coeff)
    tracers, table = lax.optimization_barrier((tracers, table))
    raw = lax.slice_in_dim(tracers, part, 2 * part, axis=2)
    raw, table = lax.optimization_barrier((raw, table))
    own.append(as_tiles(raw))
    sides.append(neighbours(own[1]))

    out = None
    for k in range(CHUNKS):
        left, right = sides[k]
        moved = transport(k, winds, left, own[k], right, (groups, count, cols * width))
        cells = exchange(moved).reshape(groups * count, cols * width)
        reacted = react(cells, *table)
        back = exchange(reacted.reshape(groups, count, cols * width))
        out = join(back, out, k)
    return from_tiles(out, (count, cols, length))


def solution(mesh):
    in_specs = (P("tracer", "region", None), P(None, "region", "tracer"), P(), P(), P(), P())
    out_specs = P("tracer", "region", None)
    return jax.shard_map(body, mesh=mesh, in_specs=in_specs, out_specs=out_specs, check_vma=False)
```
